256 devices in a mesh: uly: 32 (over y, z), blk: 8 (over x, core).
Axes of the slice: x: 4, y: 4, z: 8, core: 2. Of those that a mesh axis runs over, the one named last changes fastest.
Arguments:
- qkv: bfloat16 [65536, 6144], P(('blk', 'uly')), may hold values from -16 to 16
- tile_list: int32 [256, 8], P('blk'), may hold values from 0 to 255, as said below
Outputs:
- attended: bfloat16 [65536, 2048], P(('blk', 'uly'))
The draws below stay inside these ranges and needn't reach their ends.
Inputs may be any that keep to these rules, and one draw needn't show every extreme that they name: Let the frame of tile t be t // 32, its row t % 32 // 4 and its column t % 4. Each row of tile_list names 8 distinct tiles: its own tile and others whose frame, row and column each differ from its own by at most one.
All inputs are finite; a program needn't handle non-finite values.
Results may differ from the reference program's by a relative error of at most 0.0047.
Values may be sent and summed in bfloat16 or wider, within the bound.
No kernel may reach another device: no remote copies, remote signals or barrier semaphores. Data moves between devices by JAX's collectives and lax.ppermute only.
A program may use at most 128 MiB of HBM per device.

```python
import math
import jax
import jax.numpy as jnp
from jax import lax

HEADS = 32
HEAD_DIM = 64
TILE = 256
LISTED = 8
TCOLS = 4
TOKENS = 65536
TILES = 256
FRAME_TILES = 32


def draw_qkv(key, part):
    shape = (TOKENS, HEADS, 3, HEAD_DIM)
    values = jnp.clip(jax.random.normal(key, shape, jnp.float32), -6.0, 6.0)
    return values.reshape(TOKENS, HEADS * 3 * HEAD_DIM).astype(jnp.bfloat16)


def draw_tile_list(key, part):
    tiles = jnp.arange(TILES, dtype=jnp.int32)
    frame = tiles // FRAME_TILES
    row_of = tiles % FRAME_TILES // TCOLS
    column = tiles % TCOLS
    offsets = jnp.arange(27, dtype=jnp.int32)
    frame_step = offsets // 9 - 1
    row_step = offsets // 3 % 3 - 1
    column_step = offsets % 3 - 1
    new_frame = frame[:, None] + frame_step[None, :]
    new_row = row_of[:, None] + row_step[None, :]
    new_column = column[:, None] + column_step[None, :]
    frames = TILES // FRAME_TILES
    rows_per = FRAME_TILES // TCOLS
    valid = (new_frame >= 0) & (new_frame < frames) & (new_row >= 0) & (new_row < rows_per) & (new_column >= 0) & (new_column < TCOLS)
    neighbour = new_frame * FRAME_TILES + new_row * TCOLS + new_column
    ranking = jax.random.randint(key, (TILES, 27), 0, 2 ** 20) * 32 + offsets[None, :]
    ranking = jnp.where(valid, ranking, -1)
    ranking = jnp.where((offsets == 13)[None, :], 2 ** 30, ranking)
    _, picked = lax.top_k(ranking, LISTED)
    return jnp.take_along_axis(neighbour, picked, axis=1).astype(jnp.int32)


def setup_inputs(seed: int = 0) -> dict:
    keys = jax.random.split(jax.random.key(seed), 3)
    return {
        "qkv": draw_qkv(jax.random.fold_in(keys[2], 71), 0),
        "tile_list": draw_tile_list(jax.random.fold_in(keys[2], 71), 0),
    }


def reference(qkv, tile_list):
    score_scale = HEAD_DIM ** -0.5
    by_head = qkv.reshape(TOKENS, HEADS, 3 * HEAD_DIM)
    group_size = math.gcd(TILES, 16)
    list_groups = tile_list.reshape(TILES // group_size, group_size, LISTED)

    def one_head(head_index):
        block = lax.dynamic_index_in_dim(by_head, head_index, 1, keepdims=False).astype(jnp.float32)
        queries = block[:, :HEAD_DIM].reshape(TILES // group_size, group_size, TILE, HEAD_DIM)
        keyvals = block[:, HEAD_DIM:].reshape(TILES, TILE, 2 * HEAD_DIM)

        def run_group(inputs):
            query_part, listed = inputs
            picked = keyvals[listed]
            scores = jnp.einsum("gqd,gjkd->gqjk", query_part, picked[..., :HEAD_DIM]) * score_scale
            row_max = jnp.max(scores, axis=(2, 3), keepdims=True)
            exponent = jnp.exp(scores - row_max)
            row_sum = jnp.sum(exponent, axis=(2, 3))
            weights = lax.optimization_barrier(exponent.astype(jnp.bfloat16)).astype(jnp.float32)
            summed = jnp.einsum("gqjk,gjkd->gqd", weights, picked[..., HEAD_DIM:])
            return (summed / row_sum[..., None]).astype(jnp.bfloat16)

        result = lax.map(run_group, (queries, list_groups))
        return result.reshape(TOKENS, HEAD_DIM)

    heads_out = lax.map(one_head, jnp.arange(HEADS, dtype=jnp.int32))
    return jnp.transpose(heads_out, (1, 0, 2)).reshape(TOKENS, HEADS * HEAD_DIM)
```

```python
import jax
import jax.numpy as jnp
from jax import lax
from jax.experimental import pallas as pl
from jax.experimental.pallas import tpu as pltpu
from jax.sharding import PartitionSpec as P

HEAD_DIM = 64
PAIR = 2 * HEAD_DIM
LOG2E = 1.4426950408889634
SPLIT_HEADS = 8


def split_kernel(qkv_ref, kv_ref, q_ref):
    half = qkv_ref.shape[0] // 2
    for pair in range(kv_ref.shape[0] // 2):
        base = pair * 6 * HEAD_DIM
        for odd in range(2):
            col = base + odd * 3 * HEAD_DIM
            head = 2 * pair + odd
            kv_ref[head] = qkv_ref[:, col + HEAD_DIM : col + 3 * HEAD_DIM]
            q_ref[head] = jnp.concatenate(
                [qkv_ref[:half, col : col + HEAD_DIM], qkv_ref[half:, col : col + HEAD_DIM]], axis=1
            )


def split_heads(qkv):
    tokens, width = qkv.shape
    heads = width // (3 * HEAD_DIM)
    group = SPLIT_HEADS
    return pl.pallas_call(
        split_kernel,
        grid=(heads // group,),
        in_specs=[pl.BlockSpec((tokens, group * 3 * HEAD_DIM), lambda i: (0, i))],
        out_specs=[
            pl.BlockSpec((group, tokens, PAIR), lambda i: (i, 0, 0)),
            pl.BlockSpec((group, tokens // 2, PAIR), lambda i: (i, 0, 0)),
        ],
        out_shape=[
            jax.ShapeDtypeStruct((heads, tokens, PAIR), qkv.dtype),
            jax.ShapeDtypeStruct((heads, tokens // 2, PAIR), qkv.dtype),
        ],
        name="split_heads",
    )(qkv)


def merge_kernel(o_ref, out_ref):
    half = o_ref.shape[1]
    for pair in range(o_ref.shape[0] // 2):
        even = o_ref[2 * pair]
        odd = o_ref[2 * pair + 1]
        cols = slice(pair * PAIR, (pair + 1) * PAIR)
        out_ref[:half, cols] = jnp.concatenate([even[:, :HEAD_DIM], odd[:, :HEAD_DIM]], axis=1)
        out_ref[half:, cols] = jnp.concatenate([even[:, HEAD_DIM:], odd[:, HEAD_DIM:]], axis=1)


def merge_heads(parts):
    heads, half, _ = parts.shape
    group = SPLIT_HEADS
    return pl.pallas_call(
        merge_kernel,
        grid=(heads // group,),
        in_specs=[pl.BlockSpec((group, half, PAIR), lambda i: (i, 0, 0))],
        out_specs=pl.BlockSpec((2 * half, group * HEAD_DIM), lambda i: (0, i)),
        out_shape=jax.ShapeDtypeStruct((2 * half, heads * HEAD_DIM), parts.dtype),
        name="merge_heads",
    )(parts)


def attend_kernel(list_ref, q_ref, prev_ref, own_ref, next_ref, o_ref, raw, keys, vals, sems):
    step = pl.program_id(0)
    frame_tiles = own_ref.shape[0]
    window = 3 * frame_tiles

    @pl.when(step == 0)
    def _():
        copies = [
            pltpu.make_async_copy(src, raw.at[pl.ds(i * frame_tiles, frame_tiles)], sems.at[i])
            for i, src in enumerate((prev_ref, own_ref, next_ref))
        ]
        for copy in copies:
            copy.start()
        for copy in copies:
            copy.wait()

        def prepare(t, carry):
            kv = raw[t]
            low = lax.broadcasted_iota(jnp.int32, kv.shape, 1) < HEAD_DIM
            keys[t] = jnp.where(low, kv, pltpu.roll(kv.astype(jnp.float32), HEAD_DIM, 1).astype(kv.dtype))
            vals[t] = jnp.where(low, jnp.ones_like(kv), kv)
            return carry

        lax.fori_loop(0, window, prepare, 0)

    packed = q_ref[0].astype(jnp.float32) * (HEAD_DIM**-0.5 * LOG2E)
    scaled = jnp.concatenate([packed[:, :HEAD_DIM], packed[:, HEAD_DIM:]], axis=0)
    coarse = scaled.astype(jnp.bfloat16)
    fine = (scaled - coarse.astype(jnp.float32)).astype(jnp.bfloat16)
    query = jnp.concatenate([coarse, fine], axis=1)
    listed = [list_ref[step, j] for j in range(list_ref.shape[1])]
    scores = [
        lax.dot_general(query, keys[t], (((1,), (1,)), ((), ())), preferred_element_type=jnp.float32)
        for t in listed
    ]
    top = scores[0]
    for s in scores[1:]:
        top = jnp.maximum(top, s)
    row_max = jnp.max(top, axis=1, keepdims=True)
    total = None
    for s, t in zip(scores, listed):
        weights = jnp.exp2(s - row_max).astype(jnp.bfloat16)
        part = jnp.dot(weights, vals[t], preferred_element_type=jnp.float32)
        total = part if total is None else total + part
    out = (total[:, HEAD_DIM:] / total[:, :HEAD_DIM]).astype(o_ref.dtype)
    half = out.shape[0] // 2
    o_ref[0] = jnp.concatenate([out[:half], out[half:]], axis=1)


def attend(local_list, queries, before, own, after):
    tiles, half, _ = queries.shape
    tile_len = own.shape[1]
    hbm = pl.BlockSpec(memory_space=pl.ANY)
    window = (3 * tiles, tile_len, PAIR)
    return pl.pallas_call(
        attend_kernel,
        grid_spec=pltpu.PrefetchScalarGridSpec(
            num_scalar_prefetch=1,
            grid=(tiles,),
            in_specs=[pl.BlockSpec((1, half, PAIR), lambda i, _: (i, 0, 0)), hbm, hbm, hbm],
            out_specs=pl.BlockSpec((1, half, PAIR), lambda i, _: (i, 0, 0)),
            scratch_shapes=[
                pltpu.VMEM(window, jnp.bfloat16),
                pltpu.VMEM(window, jnp.bfloat16),
                pltpu.VMEM(window, jnp.bfloat16),
                pltpu.SemaphoreType.DMA((3,)),
            ],
        ),
        out_shape=jax.ShapeDtypeStruct(queries.shape, queries.dtype),
        compiler_params=pltpu.CompilerParams(vmem_limit_bytes=48 * 2**20),
        name="attend",
    )(local_list, queries, before, own, after)


def on_device(qkv, tile_list):
    frames = lax.axis_size("blk")
    kv, queries = split_heads(qkv)
    kv = lax.all_to_all(kv, "uly", split_axis=0, concat_axis=0, tiled=True)
    up = [(i, i + 1) for i in range(frames - 1)]
    down = [(i + 1, i) for i in range(frames - 1)]
    before = lax.ppermute(kv, "blk", up)
    after = lax.ppermute(kv, "blk", down)
    queries, kv = lax.optimization_barrier((queries, kv))
    queries = lax.all_to_all(queries, "uly", split_axis=0, concat_axis=0, tiled=True)
    local_list = tile_list - (lax.axis_index("blk") - 1) * tile_list.shape[0]
    result = attend(local_list, queries, before, kv, after)
    result = lax.all_to_all(result, "uly", split_axis=0, concat_axis=0, tiled=True)
    return merge_heads(result)


def solution(mesh):
    in_specs = (P(("blk", "uly"), None), P("blk", None))
    out_specs = P(("blk", "uly"), None)
    return jax.shard_map(
        on_device, mesh=mesh, in_specs=in_specs, out_specs=out_specs, check_vma=False
    )
```

```python
import jax
import jax.numpy as jnp
from jax import lax
from jax.experimental import pallas as pl
from jax.experimental.pallas import tpu as pltpu
from jax.sharding import PartitionSpec as P

HEAD_DIM = 64
PAIR = 2 * HEAD_DIM
SPLIT_HEADS = 16
STEP_TILES = 8


def split_kernel(qkv_ref, kv_ref, q_ref):
    half = qkv_ref.shape[0] // 2
    for pair in range(kv_ref.shape[0] // 2):
        base = pair * 6 * HEAD_DIM
        for odd in range(2):
            col = base + odd * 3 * HEAD_DIM
            head = 2 * pair + odd
            kv_ref[head] = qkv_ref[:, col + HEAD_DIM : col + 3 * HEAD_DIM]
            q_ref[head] = jnp.concatenate(
                [qkv_ref[:half, col : col + HEAD_DIM], qkv_ref[half:, col : col + HEAD_DIM]], axis=1
            )


def split_heads(qkv):
    tokens, width = qkv.shape
    heads = width // (3 * HEAD_DIM)
    group = SPLIT_HEADS
    return pl.pallas_call(
        split_kernel,
        grid=(heads // group,),
        in_specs=[pl.BlockSpec((tokens, group * 3 * HEAD_DIM), lambda i: (0, i))],
        out_specs=[
            pl.BlockSpec((group, tokens, PAIR), lambda i: (i, 0, 0)),
            pl.BlockSpec((group, tokens // 2, PAIR), lambda i: (i, 0, 0)),
        ],
        out_shape=[
            jax.ShapeDtypeStruct((heads, tokens, PAIR), qkv.dtype),
            jax.ShapeDtypeStruct((heads, tokens // 2, PAIR), qkv.dtype),
        ],
        name="split_heads",
    )(qkv)


def merge_kernel(o_ref, out_ref):
    half = o_ref.shape[1]
    for pair in range(o_ref.shape[0] // 2):
        even = o_ref[2 * pair]
        odd = o_ref[2 * pair + 1]
        cols = slice(pair * PAIR, (pair + 1) * PAIR)
        out_ref[:half, cols] = jnp.concatenate([even[:, :HEAD_DIM], odd[:, :HEAD_DIM]], axis=1)
        out_ref[half:, cols] = jnp.concatenate([even[:, HEAD_DIM:], odd[:, HEAD_DIM:]], axis=1)


def merge_heads(parts):
    heads, half, _ = parts.shape
    group = SPLIT_HEADS
    return pl.pallas_call(
        merge_kernel,
        grid=(heads // group,),
        in_specs=[pl.BlockSpec((group, half, PAIR), lambda i: (i, 0, 0))],
        out_specs=pl.BlockSpec((2 * half, group * HEAD_DIM), lambda i: (0, i)),
        out_shape=jax.ShapeDtypeStruct((2 * half, heads * HEAD_DIM), parts.dtype),
        name="merge_heads",
    )(parts)


def load_window(srcs, raw, sems):
    tiles = srcs[0].shape[0]
    copies = [
        pltpu.make_async_copy(src, raw.at[pl.ds(i * tiles, tiles)], sems.at[i])
        for i, src in enumerate(srcs)
    ]
    for copy in copies:
        copy.start()
    for copy in copies:
        copy.wait()


def padded_query(q_ref):
    packed = q_ref * jnp.bfloat16(HEAD_DIM**-0.5)
    stacked = jnp.concatenate([packed[:, :HEAD_DIM], packed[:, HEAD_DIM:]], axis=0)
    return jnp.concatenate([stacked, jnp.zeros_like(stacked)], axis=1)


def attend_kernel(list_ref, q_ref, prev_ref, own_ref, next_ref, o_ref, raw, sems):
    step = pl.program_id(0)

    @pl.when(step == 0)
    def _():
        load_window((prev_ref, own_ref, next_ref), raw, sems)

    count = list_ref.shape[1]

    def score(u):
        query = padded_query(q_ref[u])
        listed = [list_ref[step * q_ref.shape[0] + u, j] for j in range(count)]
        dims = (((1,), (1,)), ((), ()))
        scores = [
            lax.dot_general(query, raw[t], dims, preferred_element_type=jnp.float32) for t in listed
        ]
        return listed, scores

    def finish(u, listed, scores):
        top = scores[0]
        for s in scores[1:]:
            top = jnp.maximum(top, s)
        row_max = jnp.max(top, axis=1, keepdims=True)
        total = None
        for s, t in zip(scores, listed):
            weights = jnp.exp(s - row_max).astype(jnp.bfloat16)
            kv = raw[t]
            low = lax.broadcasted_iota(jnp.int32, kv.shape, 1) < HEAD_DIM
            ones_values = jnp.where(low, jnp.ones_like(kv), kv)
            part = jnp.dot(weights, ones_values, preferred_element_type=jnp.float32)
            total = part if total is None else total + part
        out = (total[:, HEAD_DIM:] / total[:, :HEAD_DIM]).astype(o_ref.dtype)
        half = out.shape[0] // 2
        o_ref[u] = jnp.concatenate([out[:half], out[half:]], axis=1)

    held = score(0)
    for u in range(q_ref.shape[0]):
        following = score(u + 1) if u + 1 < q_ref.shape[0] else None
        finish(u, *held)
        held = following


def attend(local_list, queries, before, own, after):
    tiles, half, _ = queries.shape
    tile_len = own.shape[1]
    hbm = pl.BlockSpec(memory_space=pl.ANY)
    return pl.pallas_call(
        attend_kernel,
        grid_spec=pltpu.PrefetchScalarGridSpec(
            num_scalar_prefetch=1,
            grid=(tiles // STEP_TILES,),
            in_specs=[pl.BlockSpec((STEP_TILES, half, PAIR), lambda i, _: (i, 0, 0)), hbm, hbm, hbm],
            out_specs=pl.BlockSpec((STEP_TILES, half, PAIR), lambda i, _: (i, 0, 0)),
            scratch_shapes=[
                pltpu.VMEM((3 * tiles, tile_len, PAIR), jnp.bfloat16),
                pltpu.SemaphoreType.DMA((3,)),
            ],
        ),
        out_shape=jax.ShapeDtypeStruct(queries.shape, queries.dtype),
        compiler_params=pltpu.CompilerParams(vmem_limit_bytes=48 * 2**20),
        name="attend",
    )(local_list, queries, before, own, after)


def on_device(qkv, tile_list):
    frames = lax.axis_size("blk")
    kv, queries = split_heads(qkv)
    kv = lax.all_to_all(kv, "uly", split_axis=0, concat_axis=0, tiled=True)
    up = [(i, i + 1) for i in range(frames - 1)]
    down = [(i + 1, i) for i in range(frames - 1)]
    before = lax.ppermute(kv, "blk", up)
    after = lax.ppermute(kv, "blk", down)
    queries = lax.all_to_all(queries, "uly", split_axis=0, concat_axis=0, tiled=True)
    local_list = tile_list - (lax.axis_index("blk") - 1) * tile_list.shape[0]
    result = attend(local_list, queries, before, kv, after)
    result = lax.all_to_all(result, "uly", split_axis=0, concat_axis=0, tiled=True)
    return merge_heads(result)


def solution(mesh):
    in_specs = (P(("blk", "uly"), None), P("blk", None))
    out_specs = P(("blk", "uly"), None)
    return jax.shard_map(
        on_device, mesh=mesh, in_specs=in_specs, out_specs=out_specs, check_vma=False
    )
```

```python
import jax
import jax.numpy as jnp
from jax import lax
from jax.experimental import pallas as pl
from jax.experimental.pallas import tpu as pltpu
from jax.sharding import PartitionSpec as P

HEAD_DIM = 64
PAIR = 2 * HEAD_DIM
SPLIT_HEADS = 16
STEP_TILES = 8


def split_kernel(qkv_ref, kv_ref, q_ref):
    half = qkv_ref.shape[0] // 2
    for pair in range(kv_ref.shape[0] // 2):
        base = pair * 6 * HEAD_DIM
        for odd in range(2):
            col = base + odd * 3 * HEAD_DIM
            head = 2 * pair + odd
            kv_ref[head] = qkv_ref[:, col + HEAD_DIM : col + 3 * HEAD_DIM]
            q_ref[head] = jnp.concatenate(
                [qkv_ref[:half, col : col + HEAD_DIM], qkv_ref[half:, col : col + HEAD_DIM]], axis=1
            )


def split_heads(qkv):
    tokens, width = qkv.shape
    heads = width // (3 * HEAD_DIM)
    group = SPLIT_HEADS
    return pl.pallas_call(
        split_kernel,
        grid=(heads // group,),
        in_specs=[pl.BlockSpec((tokens, group * 3 * HEAD_DIM), lambda i: (0, i))],
        out_specs=[
            pl.BlockSpec((group, tokens, PAIR), lambda i: (i, 0, 0)),
            pl.BlockSpec((group, tokens // 2, PAIR), lambda i: (i, 0, 0)),
        ],
        out_shape=[
            jax.ShapeDtypeStruct((heads, tokens, PAIR), qkv.dtype),
            jax.ShapeDtypeStruct((heads, tokens // 2, PAIR), qkv.dtype),
        ],
        name="split_heads",
    )(qkv)


def merge_kernel(o_ref, out_ref):
    half = o_ref.shape[1]
    for pair in range(o_ref.shape[0] // 2):
        even = o_ref[2 * pair]
        odd = o_ref[2 * pair + 1]
        cols = slice(pair * PAIR, (pair + 1) * PAIR)
        out_ref[:half, cols] = jnp.concatenate([even[:, :HEAD_DIM], odd[:, :HEAD_DIM]], axis=1)
        out_ref[half:, cols] = jnp.concatenate([even[:, HEAD_DIM:], odd[:, HEAD_DIM:]], axis=1)


def merge_heads(parts):
    heads, half, _ = parts.shape
    group = SPLIT_HEADS
    return pl.pallas_call(
        merge_kernel,
        grid=(heads // group,),
        in_specs=[pl.BlockSpec((group, half, PAIR), lambda i: (i, 0, 0))],
        out_specs=pl.BlockSpec((2 * half, group * HEAD_DIM), lambda i: (0, i)),
        out_shape=jax.ShapeDtypeStruct((2 * half, heads * HEAD_DIM), parts.dtype),
        compiler_params=pltpu.CompilerParams(vmem_limit_bytes=8 * 2**20),
        name="merge_heads",
    )(parts)


def load_window(srcs, raw, sems):
    tiles = srcs[0].shape[0]
    copies = [
        pltpu.make_async_copy(src, raw.at[pl.ds(i * tiles, tiles)], sems.at[i])
        for i, src in enumerate(srcs)
    ]
    for copy in copies:
        copy.start()
    for copy in copies:
        copy.wait()


def padded_query(q_ref):
    packed = q_ref * jnp.bfloat16(HEAD_DIM**-0.5)
    stacked = jnp.concatenate([packed[:, :HEAD_DIM], packed[:, HEAD_DIM:]], axis=0)
    return jnp.concatenate([stacked, jnp.zeros_like(stacked)], axis=1)


def attend_kernel(list_ref, q_ref, prev_ref, own_ref, next_ref, o_ref, raw, sems):
    step = pl.program_id(0)

    @pl.when(step == 0)
    def _():
        load_window((prev_ref, own_ref, next_ref), raw, sems)

    count = list_ref.shape[1]

    def score(u):
        query = padded_query(q_ref[u])
        listed = [list_ref[step * q_ref.shape[0] + u, j] for j in range(count)]
        dims = (((1,), (1,)), ((), ()))
        scores = [
            lax.dot_general(query, raw[t], dims, preferred_element_type=jnp.float32) for t in listed
        ]
        return listed, scores

    def finish(u, listed, scores):
        top = scores[0]
        for s in scores[1:]:
            top = jnp.maximum(top, s)
        row_max = jnp.max(top, axis=1, keepdims=True)
        total = None
        for s, t in zip(scores, listed):
            weights = jnp.exp(s - row_max).astype(jnp.bfloat16)
            kv = raw[t]
            low = lax.broadcasted_iota(jnp.int32, kv.shape, 1) < HEAD_DIM
            ones_values = jnp.where(low, jnp.ones_like(kv), kv)
            part = jnp.dot(weights, ones_values, preferred_element_type=jnp.float32)
            total = part if total is None else total + part
        out = (total[:, HEAD_DIM:] / total[:, :HEAD_DIM]).astype(o_ref.dtype)
        half = out.shape[0] // 2
        o_ref[u] = jnp.concatenate([out[:half], out[half:]], axis=1)

    held = score(0)
    for u in range(q_ref.shape[0]):
        following = score(u + 1) if u + 1 < q_ref.shape[0] else None
        finish(u, *held)
        held = following


def attend(local_list, queries, before, own, after):
    tiles, half, _ = queries.shape
    tile_len = own.shape[1]
    hbm = pl.BlockSpec(memory_space=pl.ANY)
    return pl.pallas_call(
        attend_kernel,
        grid_spec=pltpu.PrefetchScalarGridSpec(
            num_scalar_prefetch=1,
            grid=(tiles // STEP_TILES,),
            in_specs=[pl.BlockSpec((STEP_TILES, half, PAIR), lambda i, _: (i, 0, 0)), hbm, hbm, hbm],
            out_specs=pl.BlockSpec((STEP_TILES, half, PAIR), lambda i, _: (i, 0, 0)),
            scratch_shapes=[
                pltpu.VMEM((3 * tiles, tile_len, PAIR), jnp.bfloat16),
                pltpu.SemaphoreType.DMA((3,)),
            ],
        ),
        out_shape=jax.ShapeDtypeStruct(queries.shape, queries.dtype),
        compiler_params=pltpu.CompilerParams(vmem_limit_bytes=32 * 2**20),
        name="attend",
    )(local_list, queries, before, own, after)


def on_device(qkv, tile_list):
    frames = lax.axis_size("blk")
    kv, queries = split_heads(qkv)
    kv = lax.all_to_all(kv, "uly", split_axis=0, concat_axis=0, tiled=True)
    up = [(i, i + 1) for i in range(frames - 1)]
    down = [(i + 1, i) for i in range(frames - 1)]
    before = lax.ppermute(kv, "blk", up)
    after = lax.ppermute(kv, "blk", down)
    queries = lax.all_to_all(queries, "uly", split_axis=0, concat_axis=0, tiled=True)
    queries, tile_list = lax.optimization_barrier((queries, tile_list))
    local_list = tile_list - (lax.axis_index("blk") - 1) * tile_list.shape[0]
    result = attend(local_list, queries, before, kv, after)
    result = lax.all_to_all(result, "uly", split_axis=0, concat_axis=0, tiled=True)
    return merge_heads(result)


def solution(mesh):
    in_specs = (P(("blk", "uly"), None), P("blk", None))
    out_specs = P(("blk", "uly"), None)
    return jax.shard_map(
        on_device, mesh=mesh, in_specs=in_specs, out_specs=out_specs, check_vma=False
    )
```

```python
import jax
import jax.numpy as jnp
from jax import lax
from jax.experimental import pallas as pl
from jax.experimental.pallas import tpu as pltpu
from jax.sharding import PartitionSpec as P

HEAD_DIM = 64
PAIR = 2 * HEAD_DIM
SPLIT_HEADS = 16
STEP_TILES = 8


def split_kernel(qkv_ref, kv_ref, q_ref):
    half = qkv_ref.shape[0] // 2
    for pair in range(kv_ref.shape[0] // 2):
        base = pair * 6 * HEAD_DIM
        for odd in range(2):
            col = base + odd * 3 * HEAD_DIM
            head = 2 * pair + odd
            kv_ref[head] = qkv_ref[:, col + HEAD_DIM : col + 3 * HEAD_DIM]
            q_ref[head] = jnp.concatenate(
                [qkv_ref[:half, col : col + HEAD_DIM], qkv_ref[half:, col : col + HEAD_DIM]], axis=1
            )


def split_heads(qkv):
    tokens, width = qkv.shape
    heads = width // (3 * HEAD_DIM)
    group = SPLIT_HEADS
    return pl.pallas_call(
        split_kernel,
        grid=(heads // group,),
        in_specs=[pl.BlockSpec((tokens, group * 3 * HEAD_DIM), lambda i: (0, i))],
        out_specs=[
            pl.BlockSpec((group, tokens, PAIR), lambda i: (i, 0, 0)),
            pl.BlockSpec((group, tokens // 2, PAIR), lambda i: (i, 0, 0)),
        ],
        out_shape=[
            jax.ShapeDtypeStruct((heads, tokens, PAIR), qkv.dtype),
            jax.ShapeDtypeStruct((heads, tokens // 2, PAIR), qkv.dtype),
        ],
        name="split_heads",
    )(qkv)


def merge_kernel(o_ref, out_ref):
    half = o_ref.shape[1]
    for pair in range(o_ref.shape[0] // 2):
        even = o_ref[2 * pair]
        odd = o_ref[2 * pair + 1]
        cols = slice(pair * PAIR, (pair + 1) * PAIR)
        out_ref[:half, cols] = jnp.concatenate([even[:, :HEAD_DIM], odd[:, :HEAD_DIM]], axis=1)
        out_ref[half:, cols] = jnp.concatenate([even[:, HEAD_DIM:], odd[:, HEAD_DIM:]], axis=1)


def merge_heads(parts):
    heads, half, _ = parts.shape
    group = SPLIT_HEADS
    return pl.pallas_call(
        merge_kernel,
        grid=(heads // group,),
        in_specs=[pl.BlockSpec((group, half, PAIR), lambda i: (i, 0, 0))],
        out_specs=pl.BlockSpec((2 * half, group * HEAD_DIM), lambda i: (0, i)),
        out_shape=jax.ShapeDtypeStruct((2 * half, heads * HEAD_DIM), parts.dtype),
        compiler_params=pltpu.CompilerParams(vmem_limit_bytes=8 * 2**20),
        name="merge_heads",
    )(parts)


def load_window(srcs, raw, sems):
    tiles = srcs[0].shape[0]
    copies = [
        pltpu.make_async_copy(src, raw.at[pl.ds(i * tiles, tiles)], sems.at[i])
        for i, src in enumerate(srcs)
    ]
    for copy in copies:
        copy.start()
    for copy in copies:
        copy.wait()


def padded_query(q_ref):
    packed = q_ref * jnp.bfloat16(HEAD_DIM**-0.5)
    stacked = jnp.concatenate([packed[:, :HEAD_DIM], packed[:, HEAD_DIM:]], axis=0)
    return jnp.concatenate([stacked, jnp.zeros_like(stacked)], axis=1)


def attend_kernel(list_ref, q_ref, prev_ref, own_ref, next_ref, o_ref, raw, sems):
    step = pl.program_id(0)

    @pl.when(step == 0)
    def _():
        load_window((prev_ref, own_ref, next_ref), raw, sems)

    count = list_ref.shape[1]

    def score(u):
        query = padded_query(q_ref[u])
        listed = [list_ref[step * q_ref.shape[0] + u, j] for j in range(count)]
        dims = (((1,), (1,)), ((), ()))
        scores = [
            lax.dot_general(query, raw[t], dims, preferred_element_type=jnp.float32) for t in listed
        ]
        return listed, scores

    def finish(u, listed, scores):
        top = scores[0]
        for s in scores[1:]:
            top = jnp.maximum(top, s)
        row_max = jnp.max(top, axis=1, keepdims=True)
        total = None
        for s, t in zip(scores, listed):
            weights = jnp.exp(s - row_max).astype(jnp.bfloat16)
            kv = raw[t]
            low = lax.broadcasted_iota(jnp.int32, kv.shape, 1) < HEAD_DIM
            ones_values = jnp.where(low, jnp.ones_like(kv), kv)
            part = jnp.dot(weights, ones_values, preferred_element_type=jnp.float32)
            total = part if total is None else total + part
        out = (total[:, HEAD_DIM:] / total[:, :HEAD_DIM]).astype(o_ref.dtype)
        half = out.shape[0] // 2
        o_ref[u] = jnp.concatenate([out[:half], out[half:]], axis=1)

    held = score(0)
    for u in range(q_ref.shape[0]):
        following = score(u + 1) if u + 1 < q_ref.shape[0] else None
        finish(u, *held)
        held = following


def attend(local_list, queries, before, own, after):
    tiles, half, _ = queries.shape
    tile_len = own.shape[1]
    hbm = pl.BlockSpec(memory_space=pl.ANY)
    return pl.pallas_call(
        attend_kernel,
        grid_spec=pltpu.PrefetchScalarGridSpec(
            num_scalar_prefetch=1,
            grid=(tiles // STEP_TILES,),
            in_specs=[pl.BlockSpec((STEP_TILES, half, PAIR), lambda i, _: (i, 0, 0)), hbm, hbm, hbm],
            out_specs=pl.BlockSpec((STEP_TILES, half, PAIR), lambda i, _: (i, 0, 0)),
            scratch_shapes=[
                pltpu.VMEM((3 * tiles, tile_len, PAIR), jnp.bfloat16),
                pltpu.SemaphoreType.DMA((3,)),
            ],
        ),
        out_shape=jax.ShapeDtypeStruct(queries.shape, queries.dtype),
        compiler_params=pltpu.CompilerParams(vmem_limit_bytes=32 * 2**20),
        name="attend",
    )(local_list, queries, before, own, after)


def exchange(array):
    return lax.all_to_all(array, "uly", split_axis=0, concat_axis=0, tiled=True)


def on_device(qkv, tile_list):
    frames = lax.axis_size("blk")
    frame = lax.axis_index("blk")
    odd = frame % 2
    kv, queries = split_heads(qkv)
    kv = exchange(kv)
    far = lax.ppermute(kv, "blk", [p for i in range(1, frames - 1, 2) for p in ((i, i + 1), (i + 1, i))])
    near = lax.ppermute(kv, "blk", [p for i in range(0, frames, 2) for p in ((i, i + 1), (i + 1, i))])
    queries = lax.cond(odd == 0, exchange, lambda a: a, queries)
    queries, near = lax.optimization_barrier((queries, near))
    queries = lax.cond(odd == 1, exchange, lambda a: a, queries)
    frame_tiles = tile_list.shape[0]
    step = tile_list // frame_tiles - frame
    slot = 1 + jnp.where(odd == 0, step, -step)
    local_list = slot * frame_tiles + tile_list % frame_tiles
    result = attend(local_list, queries, far, kv, near)
    return merge_heads(exchange(result))


def solution(mesh):
    in_specs = (P(("blk", "uly"), None), P("blk", None))
    out_specs = P(("blk", "uly"), None)
    return jax.shard_map(
        on_device, mesh=mesh, in_specs=in_specs, out_specs=out_specs, check_vma=False
    )
```

```python
import jax
import jax.numpy as jnp
from jax import lax
from jax.experimental import pallas as pl
from jax.experimental.pallas import tpu as pltpu
from jax.sharding import PartitionSpec as P

HEAD_DIM = 64
PAIR = 2 * HEAD_DIM
SPLIT_HEADS = 16
STEP_TILES = 8
FIRST_ROWS = 8


def split_kernel(qkv_ref, kv_ref, q_ref):
    half = qkv_ref.shape[0] // 2
    for pair in range(kv_ref.shape[0] // 2):
        base = pair * 6 * HEAD_DIM
        for odd in range(2):
            col = base + odd * 3 * HEAD_DIM
            head = 2 * pair + odd
            kv_ref[head] = qkv_ref[:, col + HEAD_DIM : col + 3 * HEAD_DIM]
            q_ref[head] = jnp.concatenate(
                [qkv_ref[:half, col : col + HEAD_DIM], qkv_ref[half:, col : col + HEAD_DIM]], axis=1
            )


def split_heads(qkv):
    tokens, width = qkv.shape
    heads = width // (3 * HEAD_DIM)
    group = SPLIT_HEADS
    return pl.pallas_call(
        split_kernel,
        grid=(heads // group,),
        in_specs=[pl.BlockSpec((tokens, group * 3 * HEAD_DIM), lambda i: (0, i))],
        out_specs=[
            pl.BlockSpec((group, tokens, PAIR), lambda i: (i, 0, 0)),
            pl.BlockSpec((group, tokens // 2, PAIR), lambda i: (i, 0, 0)),
        ],
        out_shape=[
            jax.ShapeDtypeStruct((heads, tokens, PAIR), qkv.dtype),
            jax.ShapeDtypeStruct((heads, tokens // 2, PAIR), qkv.dtype),
        ],
        name="split_heads",
    )(qkv)


def merge_kernel(o_ref, out_ref):
    half = o_ref.shape[1]
    for pair in range(o_ref.shape[0] // 2):
        even = o_ref[2 * pair]
        odd = o_ref[2 * pair + 1]
        cols = slice(pair * PAIR, (pair + 1) * PAIR)
        out_ref[:half, cols] = jnp.concatenate([even[:, :HEAD_DIM], odd[:, :HEAD_DIM]], axis=1)
        out_ref[half:, cols] = jnp.concatenate([even[:, HEAD_DIM:], odd[:, HEAD_DIM:]], axis=1)


def merge_heads(parts):
    heads, half, _ = parts.shape
    group = SPLIT_HEADS
    return pl.pallas_call(
        merge_kernel,
        grid=(heads // group,),
        in_specs=[pl.BlockSpec((group, half, PAIR), lambda i: (i, 0, 0))],
        out_specs=pl.BlockSpec((2 * half, group * HEAD_DIM), lambda i: (0, i)),
        out_shape=jax.ShapeDtypeStruct((2 * half, heads * HEAD_DIM), parts.dtype),
        compiler_params=pltpu.CompilerParams(vmem_limit_bytes=8 * 2**20),
        name="merge_heads",
    )(parts)


def load_window(srcs, raw, sems):
    tiles = srcs[0].shape[0]
    copies = [
        pltpu.make_async_copy(src, raw.at[pl.ds(i * tiles, tiles)], sems.at[i])
        for i, src in enumerate(srcs)
    ]
    for copy in copies:
        copy.start()
    for copy in copies:
        copy.wait()


def padded_query(q_ref):
    packed = q_ref * jnp.bfloat16(HEAD_DIM**-0.5)
    stacked = jnp.concatenate([packed[:, :HEAD_DIM], packed[:, HEAD_DIM:]], axis=0)
    return jnp.concatenate([stacked, jnp.zeros_like(stacked)], axis=1)


def attend_kernel(list_ref, q_ref, prev_ref, own_ref, next_ref, o_ref, raw, sems):
    step = pl.program_id(0)

    @pl.when(step == 0)
    def _():
        load_window((prev_ref, own_ref, next_ref), raw, sems)

    count = list_ref.shape[1]

    def score(u):
        query = padded_query(q_ref[u])
        listed = [list_ref[step * q_ref.shape[0] + u, j] for j in range(count)]
        dims = (((1,), (1,)), ((), ()))
        scores = [
            lax.dot_general(query, raw[t], dims, preferred_element_type=jnp.float32) for t in listed
        ]
        return listed, scores

    def finish(u, listed, scores):
        top = scores[0]
        for s in scores[1:]:
            top = jnp.maximum(top, s)
        row_max = jnp.max(top, axis=1, keepdims=True)
        total = None
        for s, t in zip(scores, listed):
            weights = jnp.exp(s - row_max).astype(jnp.bfloat16)
            kv = raw[t]
            low = lax.broadcasted_iota(jnp.int32, kv.shape, 1) < HEAD_DIM
            ones_values = jnp.where(low, jnp.ones_like(kv), kv)
            part = jnp.dot(weights, ones_values, preferred_element_type=jnp.float32)
            total = part if total is None else total + part
        out = (total[:, HEAD_DIM:] / total[:, :HEAD_DIM]).astype(o_ref.dtype)
        half = out.shape[0] // 2
        o_ref[u] = jnp.concatenate([out[:half], out[half:]], axis=1)

    held = score(0)
    for u in range(q_ref.shape[0]):
        following = score(u + 1) if u + 1 < q_ref.shape[0] else None
        finish(u, *held)
        held = following


def attend(local_list, queries, before, own, after):
    tiles, half, _ = queries.shape
    tile_len = own.shape[1]
    hbm = pl.BlockSpec(memory_space=pl.ANY)
    return pl.pallas_call(
        attend_kernel,
        grid_spec=pltpu.PrefetchScalarGridSpec(
            num_scalar_prefetch=1,
            grid=(tiles // STEP_TILES,),
            in_specs=[pl.BlockSpec((STEP_TILES, half, PAIR), lambda i, _: (i, 0, 0)), hbm, hbm, hbm],
            out_specs=pl.BlockSpec((STEP_TILES, half, PAIR), lambda i, _: (i, 0, 0)),
            scratch_shapes=[
                pltpu.VMEM((3 * tiles, tile_len, PAIR), jnp.bfloat16),
                pltpu.SemaphoreType.DMA((3,)),
            ],
        ),
        out_shape=jax.ShapeDtypeStruct(queries.shape, queries.dtype),
        compiler_params=pltpu.CompilerParams(vmem_limit_bytes=32 * 2**20),
        name="attend",
    )(local_list, queries, before, own, after)


def exchange(array):
    return lax.all_to_all(array, "uly", split_axis=0, concat_axis=0, tiled=True)


def exchange_in_two(array):
    first = exchange(array[:, :FIRST_ROWS])
    array, first = lax.optimization_barrier((array, first))
    return jnp.concatenate([first, exchange(array[:, FIRST_ROWS:])], axis=1)


def on_device(qkv, tile_list):
    frames = lax.axis_size("blk")
    frame = lax.axis_index("blk")
    odd = frame % 2
    kv, queries = split_heads(qkv)
    kv = exchange(kv)
    far = lax.ppermute(kv, "blk", [p for i in range(1, frames - 1, 2) for p in ((i, i + 1), (i + 1, i))])
    near = lax.ppermute(kv, "blk", [p for i in range(0, frames, 2) for p in ((i, i + 1), (i + 1, i))])
    queries = lax.cond(odd == 0, exchange, exchange_in_two, queries)
    frame_tiles = tile_list.shape[0]
    step = tile_list // frame_tiles - frame
    slot = 1 + jnp.where(odd == 0, step, -step)
    local_list = slot * frame_tiles + tile_list % frame_tiles
    result = attend(local_list, queries, far, kv, near)
    return merge_heads(exchange(result))


def solution(mesh):
    in_specs = (P(("blk", "uly"), None), P("blk", None))
    out_specs = P(("blk", "uly"), None)
    return jax.shard_map(
        on_device, mesh=mesh, in_specs=in_specs, out_specs=out_specs, check_vma=False
    )
```

```python
import jax
import jax.numpy as jnp
from jax import lax
from jax.experimental import pallas as pl
from jax.experimental.pallas import tpu as pltpu
from jax.sharding import PartitionSpec as P

HEAD_DIM = 64
PAIR = 2 * HEAD_DIM
SPLIT_HEADS = 16
STEP_TILES = 16
Z_DEVICES = 8


def split_kernel(qkv_ref, kv_ref, q_ref):
    half = qkv_ref.shape[0] // 2
    for pair in range(kv_ref.shape[0] // 2):
        base = pair * 6 * HEAD_DIM
        for odd in range(2):
            col = base + odd * 3 * HEAD_DIM
            head = 2 * pair + odd
            kv_ref[head] = qkv_ref[:, col + HEAD_DIM : col + 3 * HEAD_DIM]
            q_ref[head] = jnp.concatenate(
                [qkv_ref[:half, col : col + HEAD_DIM], qkv_ref[half:, col : col + HEAD_DIM]], axis=1
            )


def split_heads(qkv):
    tokens, width = qkv.shape
    heads = width // (3 * HEAD_DIM)
    group = SPLIT_HEADS
    return pl.pallas_call(
        split_kernel,
        grid=(heads // group,),
        in_specs=[pl.BlockSpec((tokens, group * 3 * HEAD_DIM), lambda i: (0, i))],
        out_specs=[
            pl.BlockSpec((group, tokens, PAIR), lambda i: (i, 0, 0)),
            pl.BlockSpec((group, tokens // 2, PAIR), lambda i: (i, 0, 0)),
        ],
        out_shape=[
            jax.ShapeDtypeStruct((heads, tokens, PAIR), qkv.dtype),
            jax.ShapeDtypeStruct((heads, tokens // 2, PAIR), qkv.dtype),
        ],
        name="split_heads",
    )(qkv)


def merge_kernel(o_ref, out_ref):
    half = o_ref.shape[1]
    for pair in range(o_ref.shape[0] // 2):
        even = o_ref[2 * pair]
        odd = o_ref[2 * pair + 1]
        cols = slice(pair * PAIR, (pair + 1) * PAIR)
        out_ref[:half, cols] = jnp.concatenate([even[:, :HEAD_DIM], odd[:, :HEAD_DIM]], axis=1)
        out_ref[half:, cols] = jnp.concatenate([even[:, HEAD_DIM:], odd[:, HEAD_DIM:]], axis=1)


def merge_heads(parts):
    heads, half, _ = parts.shape
    group = SPLIT_HEADS
    return pl.pallas_call(
        merge_kernel,
        grid=(heads // group,),
        in_specs=[pl.BlockSpec((group, half, PAIR), lambda i: (i, 0, 0))],
        out_specs=pl.BlockSpec((2 * half, group * HEAD_DIM), lambda i: (0, i)),
        out_shape=jax.ShapeDtypeStruct((2 * half, heads * HEAD_DIM), parts.dtype),
        compiler_params=pltpu.CompilerParams(vmem_limit_bytes=8 * 2**20),
        name="merge_heads",
    )(parts)


def load_all(pairs, sems):
    copies = [pltpu.make_async_copy(src, dst, sems.at[i]) for i, (src, dst) in enumerate(pairs)]
    for copy in copies:
        copy.start()
    for copy in copies:
        copy.wait()


def padded_query(packed):
    packed = packed * jnp.bfloat16(HEAD_DIM**-0.5)
    stacked = jnp.concatenate([packed[:, :HEAD_DIM], packed[:, HEAD_DIM:]], axis=0)
    return jnp.concatenate([stacked, jnp.zeros_like(stacked)], axis=1)


def attend_kernel(list_ref, q_ref, prev_ref, own_ref, next_ref, o_ref, asked, raw, sems):
    step = pl.program_id(0)

    @pl.when(step == 0)
    def _():
        tiles = own_ref.shape[0]
        pairs = [
            (src, raw.at[pl.ds(i * tiles, tiles)])
            for i, src in enumerate((prev_ref, own_ref, next_ref))
        ]
        pairs.append((q_ref, asked))
        load_all(pairs, sems)

    count = list_ref.shape[1] - 1

    def score(u):
        tile = step * o_ref.shape[0] + u
        query = padded_query(asked[list_ref[tile, count]])
        listed = [list_ref[tile, j] for j in range(count)]
        dims = (((1,), (1,)), ((), ()))
        scores = [
            lax.dot_general(query, raw[t], dims, preferred_element_type=jnp.float32) for t in listed
        ]
        return listed, scores

    def finish(u, listed, scores):
        top = scores[0]
        for s in scores[1:]:
            top = jnp.maximum(top, s)
        row_max = jnp.max(top, axis=1, keepdims=True)
        total = None
        for s, t in zip(scores, listed):
            weights = jnp.exp(s - row_max).astype(jnp.bfloat16)
            kv = raw[t]
            low = lax.broadcasted_iota(jnp.int32, kv.shape, 1) < HEAD_DIM
            ones_values = jnp.where(low, jnp.ones_like(kv), kv)
            part = jnp.dot(weights, ones_values, preferred_element_type=jnp.float32)
            total = part if total is None else total + part
        out = (total[:, HEAD_DIM:] / total[:, :HEAD_DIM]).astype(o_ref.dtype)
        half = out.shape[0] // 2
        o_ref[u] = jnp.concatenate([out[:half], out[half:]], axis=1)

    held = score(0)
    for u in range(o_ref.shape[0]):
        following = score(u + 1) if u + 1 < o_ref.shape[0] else None
        finish(u, *held)
        held = following


def attend(local_list, queries, before, own, after):
    tiles, half, _ = queries.shape
    tile_len = own.shape[1]
    hbm = pl.BlockSpec(memory_space=pl.ANY)
    return pl.pallas_call(
        attend_kernel,
        grid_spec=pltpu.PrefetchScalarGridSpec(
            num_scalar_prefetch=1,
            grid=(tiles // STEP_TILES,),
            in_specs=[hbm] * 4,
            out_specs=pl.BlockSpec((STEP_TILES, half, PAIR), lambda i, _: (i, 0, 0)),
            scratch_shapes=[
                pltpu.VMEM((tiles, half, PAIR), jnp.bfloat16),
                pltpu.VMEM((3 * tiles, tile_len, PAIR), jnp.bfloat16),
                pltpu.SemaphoreType.DMA((4,)),
            ],
        ),
        out_shape=jax.ShapeDtypeStruct((tiles, half, PAIR), queries.dtype),
        compiler_params=pltpu.CompilerParams(vmem_limit_bytes=32 * 2**20),
        name="attend",
    )(local_list, queries, before, own, after)


def exchange(array):
    return lax.all_to_all(array, ("y", "z"), split_axis=0, concat_axis=0, tiled=True)


def exchange_by_axis(array):
    y, z = lax.axis_size("y"), lax.axis_size("z")
    parts = array.reshape((y, z) + array.shape[1:])
    parts = lax.all_to_all(parts, "y", split_axis=0, concat_axis=0, tiled=True)
    parts = jnp.swapaxes(parts, 0, 1)
    parts = lax.all_to_all(parts, "z", split_axis=0, concat_axis=0, tiled=True)
    return parts.reshape(array.shape)


def on_device(qkv, tile_list):
    frames = lax.axis_size("blk")
    frame = lax.axis_index("blk")
    odd = frame % 2
    kv, queries = split_heads(qkv)
    kv = exchange(kv)
    far = lax.ppermute(kv, "blk", [p for i in range(1, frames - 1, 2) for p in ((i, i + 1), (i + 1, i))])
    near = lax.ppermute(kv, "blk", [p for i in range(0, frames, 2) for p in ((i, i + 1), (i + 1, i))])
    frame_tiles = tile_list.shape[0]
    step = tile_list // frame_tiles - frame
    slot = 1 - jnp.where(odd == 0, step, -step)
    listed = slot * frame_tiles + tile_list % frame_tiles
    tiles = lax.broadcasted_iota(jnp.int32, (frame_tiles, 1), 0)
    y, z = lax.axis_size("y"), lax.axis_size("z")
    order = jnp.where(odd == 0, tiles, tiles % z * y + tiles // z)
    local_list = jnp.concatenate([listed, order], axis=1)
    queries, local_list = lax.optimization_barrier((queries, local_list))
    queries = lax.cond(odd == 0, exchange, exchange_by_axis, queries)
    result = attend(local_list, queries, near, kv, far)
    return merge_heads(exchange(result))


def solution(mesh):
    ring = Z_DEVICES
    axes = mesh.devices.reshape(mesh.devices.shape[0] // ring, ring, mesh.devices.shape[1])
    mesh = jax.sharding.Mesh(axes, ("y", "z", "blk"))
    in_specs = (P(("blk", "y", "z"), None), P("blk", None))
    out_specs = P(("blk", "y", "z"), None)
    return jax.shard_map(
        on_device, mesh=mesh, in_specs=in_specs, out_specs=out_specs, check_vma=False
    )
```

```python
import jax
import jax.numpy as jnp
from jax import lax
from jax.experimental import pallas as pl
from jax.experimental.pallas import tpu as pltpu
from jax.sharding import PartitionSpec as P

HEAD_DIM = 64
PAIR = 2 * HEAD_DIM
SPLIT_HEADS = 16
STEP_TILES = 16
Z_DEVICES = 8


def split_kernel(qkv_ref, kv_ref, q_ref):
    half = qkv_ref.shape[0] // 2
    for pair in range(kv_ref.shape[0] // 2):
        base = pair * 6 * HEAD_DIM
        for odd in range(2):
            col = base + odd * 3 * HEAD_DIM
            head = 2 * pair + odd
            kv_ref[head] = qkv_ref[:, col + HEAD_DIM : col + 3 * HEAD_DIM]
            q_ref[head] = jnp.concatenate(
                [qkv_ref[:half, col : col + HEAD_DIM], qkv_ref[half:, col : col + HEAD_DIM]], axis=1
            )


def split_heads(qkv):
    tokens, width = qkv.shape
    heads = width // (3 * HEAD_DIM)
    group = SPLIT_HEADS
    return pl.pallas_call(
        split_kernel,
        grid=(heads // group,),
        in_specs=[pl.BlockSpec((tokens, group * 3 * HEAD_DIM), lambda i: (0, i))],
        out_specs=[
            pl.BlockSpec((group, tokens, PAIR), lambda i: (i, 0, 0)),
            pl.BlockSpec((group, tokens // 2, PAIR), lambda i: (i, 0, 0)),
        ],
        out_shape=[
            jax.ShapeDtypeStruct((heads, tokens, PAIR), qkv.dtype),
            jax.ShapeDtypeStruct((heads, tokens // 2, PAIR), qkv.dtype),
        ],
        name="split_heads",
    )(qkv)


def merge_kernel(o_ref, out_ref):
    half = o_ref.shape[1]
    for pair in range(o_ref.shape[0] // 2):
        even = o_ref[2 * pair]
        odd = o_ref[2 * pair + 1]
        cols = slice(pair * PAIR, (pair + 1) * PAIR)
        out_ref[:half, cols] = jnp.concatenate([even[:, :HEAD_DIM], odd[:, :HEAD_DIM]], axis=1)
        out_ref[half:, cols] = jnp.concatenate([even[:, HEAD_DIM:], odd[:, HEAD_DIM:]], axis=1)


def merge_heads(parts):
    heads, half, _ = parts.shape
    group = SPLIT_HEADS
    return pl.pallas_call(
        merge_kernel,
        grid=(heads // group,),
        in_specs=[pl.BlockSpec((group, half, PAIR), lambda i: (i, 0, 0))],
        out_specs=pl.BlockSpec((2 * half, group * HEAD_DIM), lambda i: (0, i)),
        out_shape=jax.ShapeDtypeStruct((2 * half, heads * HEAD_DIM), parts.dtype),
        compiler_params=pltpu.CompilerParams(vmem_limit_bytes=8 * 2**20),
        name="merge_heads",
    )(parts)


def load_all(pairs, sems):
    copies = [pltpu.make_async_copy(src, dst, sems.at[i]) for i, (src, dst) in enumerate(pairs)]
    for copy in copies:
        copy.start()
    for copy in copies:
        copy.wait()


def padded_query(packed):
    packed = packed * jnp.bfloat16(HEAD_DIM**-0.5)
    stacked = jnp.concatenate([packed[:, :HEAD_DIM], packed[:, HEAD_DIM:]], axis=0)
    return jnp.concatenate([stacked, jnp.zeros_like(stacked)], axis=1)


def attend_kernel(list_ref, q_ref, prev_ref, own_ref, next_ref, o_ref, asked, raw, sems):
    step = pl.program_id(0)

    @pl.when(step == 0)
    def _():
        tiles = own_ref.shape[0]
        pairs = [
            (src, raw.at[pl.ds(i * tiles, tiles)])
            for i, src in enumerate((prev_ref, own_ref, next_ref))
        ]
        pairs.append((q_ref, asked))
        load_all(pairs, sems)

    count = list_ref.shape[1]

    def score(u):
        tile = step * o_ref.shape[0] + u
        query = padded_query(asked[tile])
        listed = [list_ref[tile, j] for j in range(count)]
        dims = (((1,), (1,)), ((), ()))
        scores = [
            lax.dot_general(query, raw[t], dims, preferred_element_type=jnp.float32) for t in listed
        ]
        return listed, scores

    def finish(u, listed, scores):
        top = scores[0]
        for s in scores[1:]:
            top = jnp.maximum(top, s)
        row_max = jnp.max(top, axis=1, keepdims=True)
        total = None
        for s, t in zip(scores, listed):
            weights = jnp.exp(s - row_max).astype(jnp.bfloat16)
            kv = raw[t]
            low = lax.broadcasted_iota(jnp.int32, kv.shape, 1) < HEAD_DIM
            ones_values = jnp.where(low, jnp.ones_like(kv), kv)
            part = jnp.dot(weights, ones_values, preferred_element_type=jnp.float32)
            total = part if total is None else total + part
        out = (total[:, HEAD_DIM:] / total[:, :HEAD_DIM]).astype(o_ref.dtype)
        half = out.shape[0] // 2
        o_ref[u] = jnp.concatenate([out[:half], out[half:]], axis=1)

    held = score(0)
    for u in range(o_ref.shape[0]):
        following = score(u + 1) if u + 1 < o_ref.shape[0] else None
        finish(u, *held)
        held = following


def attend(local_list, queries, before, own, after):
    tiles, half, _ = queries.shape
    tile_len = own.shape[1]
    hbm = pl.BlockSpec(memory_space=pl.ANY)
    return pl.pallas_call(
        attend_kernel,
        grid_spec=pltpu.PrefetchScalarGridSpec(
            num_scalar_prefetch=1,
            grid=(tiles // STEP_TILES,),
            in_specs=[hbm] * 4,
            out_specs=pl.BlockSpec((STEP_TILES, half, PAIR), lambda i, _: (i, 0, 0)),
            scratch_shapes=[
                pltpu.VMEM((tiles, half, PAIR), jnp.bfloat16),
                pltpu.VMEM((3 * tiles, tile_len, PAIR), jnp.bfloat16),
                pltpu.SemaphoreType.DMA((4,)),
            ],
        ),
        out_shape=jax.ShapeDtypeStruct((tiles, half, PAIR), queries.dtype),
        compiler_params=pltpu.CompilerParams(vmem_limit_bytes=32 * 2**20),
        name="attend",
    )(local_list, queries, before, own, after)


def exchange(array):
    return lax.all_to_all(array, ("y", "z"), split_axis=0, concat_axis=0, tiled=True)


def exchange_by_axis(array):
    y, z = lax.axis_size("y"), lax.axis_size("z")
    parts = array.reshape((y, z) + array.shape[1:])
    parts = lax.all_to_all(parts, "y", split_axis=0, concat_axis=0, tiled=True)
    parts = jnp.swapaxes(parts, 0, 1)
    parts = lax.all_to_all(parts, "z", split_axis=0, concat_axis=0, tiled=True)
    return parts.reshape(array.shape)


def late_frame(frame):
    return (frame + 1) // 2 % 2


def on_device(qkv, tile_list):
    frames = lax.axis_size("blk")
    frame = lax.axis_index("blk")
    kv, queries = split_heads(qkv)
    kv = lax.cond(late_frame(frame) == 0, exchange, exchange_by_axis, kv)
    far = lax.ppermute(kv, "blk", [p for i in range(1, frames - 1, 2) for p in ((i, i + 1), (i + 1, i))])
    queries = exchange(queries)
    near = lax.ppermute(kv, "blk", [p for i in range(0, frames, 2) for p in ((i, i + 1), (i + 1, i))])
    far, queries, tile_list = lax.optimization_barrier((far, queries, tile_list))
    frame_tiles = tile_list.shape[0]
    their_frame, place = tile_list // frame_tiles, tile_list % frame_tiles
    step = their_frame - frame
    slot = 1 - jnp.where(frame % 2 == 0, step, -step)
    y, z = lax.axis_size("y"), lax.axis_size("z")
    place = jnp.where(late_frame(their_frame) == 0, place, place % z * y + place // z)
    local_list = slot * frame_tiles + place
    result = attend(local_list, queries, near, kv, far)
    return merge_heads(exchange(result))


def solution(mesh):
    ring = Z_DEVICES
    axes = mesh.devices.reshape(mesh.devices.shape[0] // ring, ring, mesh.devices.shape[1])
    mesh = jax.sharding.Mesh(axes, ("y", "z", "blk"))
    in_specs = (P(("blk", "y", "z"), None), P("blk", None))
    out_specs = P(("blk", "y", "z"), None)
    return jax.shard_map(
        on_device, mesh=mesh, in_specs=in_specs, out_specs=out_specs, check_vma=False
    )
```

```python
import jax
import jax.numpy as jnp
from jax import lax
from jax.experimental import pallas as pl
from jax.experimental.pallas import tpu as pltpu
from jax.sharding import PartitionSpec as P

HEAD_DIM = 64
PAIR = 2 * HEAD_DIM
SPLIT_HEADS = 16
STEP_TILES = 16
FIRST_ROWS = 8


def split_kernel(qkv_ref, kv_ref, q_ref):
    half = qkv_ref.shape[0] // 2
    for pair in range(kv_ref.shape[0] // 2):
        base = pair * 6 * HEAD_DIM
        for odd in range(2):
            col = base + odd * 3 * HEAD_DIM
            head = 2 * pair + odd
            kv_ref[head] = qkv_ref[:, col + HEAD_DIM : col + 3 * HEAD_DIM]
            q_ref[head] = jnp.concatenate(
                [qkv_ref[:half, col : col + HEAD_DIM], qkv_ref[half:, col : col + HEAD_DIM]], axis=1
            )


def split_heads(qkv):
    tokens, width = qkv.shape
    heads = width // (3 * HEAD_DIM)
    group = SPLIT_HEADS
    return pl.pallas_call(
        split_kernel,
        grid=(heads // group,),
        in_specs=[pl.BlockSpec((tokens, group * 3 * HEAD_DIM), lambda i: (0, i))],
        out_specs=[
            pl.BlockSpec((group, tokens, PAIR), lambda i: (i, 0, 0)),
            pl.BlockSpec((group, tokens // 2, PAIR), lambda i: (i, 0, 0)),
        ],
        out_shape=[
            jax.ShapeDtypeStruct((heads, tokens, PAIR), qkv.dtype),
            jax.ShapeDtypeStruct((heads, tokens // 2, PAIR), qkv.dtype),
        ],
        name="split_heads",
    )(qkv)


def merge_kernel(o_ref, out_ref):
    half = o_ref.shape[1]
    for pair in range(o_ref.shape[0] // 2):
        even = o_ref[2 * pair]
        odd = o_ref[2 * pair + 1]
        cols = slice(pair * PAIR, (pair + 1) * PAIR)
        out_ref[:half, cols] = jnp.concatenate([even[:, :HEAD_DIM], odd[:, :HEAD_DIM]], axis=1)
        out_ref[half:, cols] = jnp.concatenate([even[:, HEAD_DIM:], odd[:, HEAD_DIM:]], axis=1)


def merge_heads(parts):
    heads, half, _ = parts.shape
    group = SPLIT_HEADS
    return pl.pallas_call(
        merge_kernel,
        grid=(heads // group,),
        in_specs=[pl.BlockSpec((group, half, PAIR), lambda i: (i, 0, 0))],
        out_specs=pl.BlockSpec((2 * half, group * HEAD_DIM), lambda i: (0, i)),
        out_shape=jax.ShapeDtypeStruct((2 * half, heads * HEAD_DIM), parts.dtype),
        compiler_params=pltpu.CompilerParams(vmem_limit_bytes=8 * 2**20),
        name="merge_heads",
    )(parts)


def load_all(pairs, sems):
    copies = [pltpu.make_async_copy(src, dst, sems.at[i]) for i, (src, dst) in enumerate(pairs)]
    for copy in copies:
        copy.start()
    for copy in copies:
        copy.wait()


def padded_query(packed):
    packed = packed * jnp.bfloat16(HEAD_DIM**-0.5)
    stacked = jnp.concatenate([packed[:, :HEAD_DIM], packed[:, HEAD_DIM:]], axis=0)
    return jnp.concatenate([stacked, jnp.zeros_like(stacked)], axis=1)


def attend_kernel(list_ref, q_ref, prev_ref, own_ref, next_ref, o_ref, asked, raw, sems):
    step = pl.program_id(0)

    @pl.when(step == 0)
    def _():
        tiles = own_ref.shape[0]
        pairs = [
            (src, raw.at[pl.ds(i * tiles, tiles)])
            for i, src in enumerate((prev_ref, own_ref, next_ref))
        ]
        pairs.append((q_ref, asked))
        load_all(pairs, sems)

    count = list_ref.shape[1]

    def score(u):
        tile = step * o_ref.shape[0] + u
        query = padded_query(asked[tile])
        listed = [list_ref[tile, j] for j in range(count)]
        dims = (((1,), (1,)), ((), ()))
        scores = [
            lax.dot_general(query, raw[t], dims, preferred_element_type=jnp.float32) for t in listed
        ]
        return listed, scores

    def finish(u, listed, scores):
        top = scores[0]
        for s in scores[1:]:
            top = jnp.maximum(top, s)
        row_max = jnp.max(top, axis=1, keepdims=True)
        total = None
        for s, t in zip(scores, listed):
            weights = jnp.exp(s - row_max).astype(jnp.bfloat16)
            kv = raw[t]
            low = lax.broadcasted_iota(jnp.int32, kv.shape, 1) < HEAD_DIM
            ones_values = jnp.where(low, jnp.ones_like(kv), kv)
            part = jnp.dot(weights, ones_values, preferred_element_type=jnp.float32)
            total = part if total is None else total + part
        out = (total[:, HEAD_DIM:] / total[:, :HEAD_DIM]).astype(o_ref.dtype)
        half = out.shape[0] // 2
        o_ref[u] = jnp.concatenate([out[:half], out[half:]], axis=1)

    held = score(0)
    for u in range(o_ref.shape[0]):
        following = score(u + 1) if u + 1 < o_ref.shape[0] else None
        finish(u, *held)
        held = following


def attend(local_list, queries, before, own, after):
    tiles, half, _ = queries.shape
    tile_len = own.shape[1]
    hbm = pl.BlockSpec(memory_space=pl.ANY)
    return pl.pallas_call(
        attend_kernel,
        grid_spec=pltpu.PrefetchScalarGridSpec(
            num_scalar_prefetch=1,
            grid=(tiles // STEP_TILES,),
            in_specs=[hbm] * 4,
            out_specs=pl.BlockSpec((STEP_TILES, half, PAIR), lambda i, _: (i, 0, 0)),
            scratch_shapes=[
                pltpu.VMEM((tiles, half, PAIR), jnp.bfloat16),
                pltpu.VMEM((3 * tiles, tile_len, PAIR), jnp.bfloat16),
                pltpu.SemaphoreType.DMA((4,)),
            ],
        ),
        out_shape=jax.ShapeDtypeStruct((tiles, half, PAIR), queries.dtype),
        compiler_params=pltpu.CompilerParams(vmem_limit_bytes=32 * 2**20),
        name="attend",
    )(local_list, queries, before, own, after)


def exchange(array):
    return lax.all_to_all(array, "uly", split_axis=0, concat_axis=0, tiled=True)


def exchange_in_two(array):
    first = exchange(array[:, :FIRST_ROWS])
    array, first = lax.optimization_barrier((array, first))
    return jnp.concatenate([first, exchange(array[:, FIRST_ROWS:])], axis=1)


def late_frame(frame):
    return (frame + 1) // 2 % 2


def on_device(qkv, tile_list):
    frames = lax.axis_size("blk")
    frame = lax.axis_index("blk")
    kv, queries = split_heads(qkv)
    kv = lax.cond(late_frame(frame) == 0, exchange, exchange_in_two, kv)
    far = lax.ppermute(kv, "blk", [p for i in range(1, frames - 1, 2) for p in ((i, i + 1), (i + 1, i))])
    queries = exchange(queries)
    near = lax.ppermute(kv, "blk", [p for i in range(0, frames, 2) for p in ((i, i + 1), (i + 1, i))])
    far, queries, tile_list = lax.optimization_barrier((far, queries, tile_list))
    frame_tiles = tile_list.shape[0]
    their_frame, place = tile_list // frame_tiles, tile_list % frame_tiles
    step = their_frame - frame
    slot = 1 - jnp.where(frame % 2 == 0, step, -step)
    local_list = slot * frame_tiles + place
    result = attend(local_list, queries, near, kv, far)
    return merge_heads(exchange(result))


def solution(mesh):
    in_specs = (P(("blk", "uly"), None), P("blk", None))
    out_specs = P(("blk", "uly"), None)
    return jax.shard_map(
        on_device, mesh=mesh, in_specs=in_specs, out_specs=out_specs, check_vma=False
    )
```

```python
import jax
import jax.numpy as jnp
from jax import lax
from jax.experimental import pallas as pl
from jax.experimental.pallas import tpu as pltpu
from jax.sharding import PartitionSpec as P

HEAD_DIM = 64
PAIR = 2 * HEAD_DIM
SPLIT_HEADS = 16
STEP_TILES = 16
FIRST_ROWS = 8


def split_kernel(qkv_ref, kv_ref, first_ref, rest_ref):
    half = qkv_ref.shape[0] // 2
    for pair in range(kv_ref.shape[0] // 2):
        base = pair * 6 * HEAD_DIM
        for odd in range(2):
            col = base + odd * 3 * HEAD_DIM
            head = 2 * pair + odd
            kv_ref[head] = qkv_ref[:, col + HEAD_DIM : col + 3 * HEAD_DIM]
            packed = jnp.concatenate(
                [qkv_ref[:half, col : col + HEAD_DIM], qkv_ref[half:, col : col + HEAD_DIM]], axis=1
            )
            first_ref[head] = packed[:FIRST_ROWS]
            rest_ref[head] = packed[FIRST_ROWS:]


def split_heads(qkv):
    tokens, width = qkv.shape
    heads = width // (3 * HEAD_DIM)
    group = SPLIT_HEADS
    return pl.pallas_call(
        split_kernel,
        grid=(heads // group,),
        in_specs=[pl.BlockSpec((tokens, group * 3 * HEAD_DIM), lambda i: (0, i))],
        out_specs=[
            pl.BlockSpec((group, tokens, PAIR), lambda i: (i, 0, 0)),
            pl.BlockSpec((group, FIRST_ROWS, PAIR), lambda i: (i, 0, 0)),
            pl.BlockSpec((group, tokens // 2 - FIRST_ROWS, PAIR), lambda i: (i, 0, 0)),
        ],
        out_shape=[
            jax.ShapeDtypeStruct((heads, tokens, PAIR), qkv.dtype),
            jax.ShapeDtypeStruct((heads, FIRST_ROWS, PAIR), qkv.dtype),
            jax.ShapeDtypeStruct((heads, tokens // 2 - FIRST_ROWS, PAIR), qkv.dtype),
        ],
        name="split_heads",
    )(qkv)


def merge_kernel(o_ref, out_ref):
    half = o_ref.shape[1]
    for pair in range(o_ref.shape[0] // 2):
        even = o_ref[2 * pair]
        odd = o_ref[2 * pair + 1]
        cols = slice(pair * PAIR, (pair + 1) * PAIR)
        out_ref[:half, cols] = jnp.concatenate([even[:, :HEAD_DIM], odd[:, :HEAD_DIM]], axis=1)
        out_ref[half:, cols] = jnp.concatenate([even[:, HEAD_DIM:], odd[:, HEAD_DIM:]], axis=1)


def merge_heads(parts):
    heads, half, _ = parts.shape
    group = SPLIT_HEADS
    return pl.pallas_call(
        merge_kernel,
        grid=(heads // group,),
        in_specs=[pl.BlockSpec((group, half, PAIR), lambda i: (i, 0, 0))],
        out_specs=pl.BlockSpec((2 * half, group * HEAD_DIM), lambda i: (0, i)),
        out_shape=jax.ShapeDtypeStruct((2 * half, heads * HEAD_DIM), parts.dtype),
        compiler_params=pltpu.CompilerParams(vmem_limit_bytes=8 * 2**20),
        name="merge_heads",
    )(parts)


def load_all(pairs, sems):
    copies = [pltpu.make_async_copy(src, dst, sems.at[i]) for i, (src, dst) in enumerate(pairs)]
    for copy in copies:
        copy.start()
    for copy in copies:
        copy.wait()


def padded_query(packed):
    packed = packed * jnp.bfloat16(HEAD_DIM**-0.5)
    stacked = jnp.concatenate([packed[:, :HEAD_DIM], packed[:, HEAD_DIM:]], axis=0)
    return jnp.concatenate([stacked, jnp.zeros_like(stacked)], axis=1)


def attend_kernel(
    list_ref, first_ref, rest_ref, prev_ref, own_ref, next_ref, o_ref, asked, raw, sems
):
    step = pl.program_id(0)

    @pl.when(step == 0)
    def _():
        tiles = own_ref.shape[0]
        pairs = [
            (src, raw.at[pl.ds(i * tiles, tiles)])
            for i, src in enumerate((prev_ref, own_ref, next_ref))
        ]
        rows = first_ref.shape[1]
        pairs.append((first_ref, asked.at[:, pl.ds(0, rows)]))
        pairs.append((rest_ref, asked.at[:, pl.ds(rows, rest_ref.shape[1])]))
        load_all(pairs, sems)

    count = list_ref.shape[1]

    def score(u):
        tile = step * o_ref.shape[0] + u
        query = padded_query(asked[tile])
        listed = [list_ref[tile, j] for j in range(count)]
        dims = (((1,), (1,)), ((), ()))
        scores = [
            lax.dot_general(query, raw[t], dims, preferred_element_type=jnp.float32) for t in listed
        ]
        return listed, scores

    def finish(u, listed, scores):
        top = scores[0]
        for s in scores[1:]:
            top = jnp.maximum(top, s)
        row_max = jnp.max(top, axis=1, keepdims=True)
        total = None
        for s, t in zip(scores, listed):
            weights = jnp.exp(s - row_max).astype(jnp.bfloat16)
            kv = raw[t]
            low = lax.broadcasted_iota(jnp.int32, kv.shape, 1) < HEAD_DIM
            ones_values = jnp.where(low, jnp.ones_like(kv), kv)
            part = jnp.dot(weights, ones_values, preferred_element_type=jnp.float32)
            total = part if total is None else total + part
        out = (total[:, HEAD_DIM:] / total[:, :HEAD_DIM]).astype(o_ref.dtype)
        half = out.shape[0] // 2
        o_ref[u] = jnp.concatenate([out[:half], out[half:]], axis=1)

    held = score(0)
    for u in range(o_ref.shape[0]):
        following = score(u + 1) if u + 1 < o_ref.shape[0] else None
        finish(u, *held)
        held = following


def attend(local_list, first, rest, before, own, after):
    tiles, half = first.shape[0], first.shape[1] + rest.shape[1]
    tile_len = own.shape[1]
    hbm = pl.BlockSpec(memory_space=pl.ANY)
    return pl.pallas_call(
        attend_kernel,
        grid_spec=pltpu.PrefetchScalarGridSpec(
            num_scalar_prefetch=1,
            grid=(tiles // STEP_TILES,),
            in_specs=[hbm] * 5,
            out_specs=pl.BlockSpec((STEP_TILES, half, PAIR), lambda i, _: (i, 0, 0)),
            scratch_shapes=[
                pltpu.VMEM((tiles, half, PAIR), jnp.bfloat16),
                pltpu.VMEM((3 * tiles, tile_len, PAIR), jnp.bfloat16),
                pltpu.SemaphoreType.DMA((5,)),
            ],
        ),
        out_shape=jax.ShapeDtypeStruct((tiles, half, PAIR), rest.dtype),
        compiler_params=pltpu.CompilerParams(vmem_limit_bytes=32 * 2**20),
        name="attend",
    )(local_list, first, rest, before, own, after)


def exchange(array):
    return lax.all_to_all(array, "uly", split_axis=0, concat_axis=0, tiled=True)


def send_early(kv, first):
    tokens = kv.shape[1]
    both = exchange(jnp.concatenate([kv, first], axis=1))
    return both[:, :tokens], both[:, tokens:]


def send_late(kv, first):
    first = exchange(first)
    kv, first = lax.optimization_barrier((kv, first))
    return exchange(kv), first


def late_frame(frame):
    return (frame + 1) // 2 % 2


def on_device(qkv, tile_list):
    frames = lax.axis_size("blk")
    frame = lax.axis_index("blk")
    kv, first, rest = split_heads(qkv)
    kv, first = lax.cond(late_frame(frame) == 0, send_early, send_late, kv, first)
    far = lax.ppermute(kv, "blk", [p for i in range(1, frames - 1, 2) for p in ((i, i + 1), (i + 1, i))])
    rest = exchange(rest)
    near = lax.ppermute(kv, "blk", [p for i in range(0, frames, 2) for p in ((i, i + 1), (i + 1, i))])
    far, rest, tile_list = lax.optimization_barrier((far, rest, tile_list))
    frame_tiles = tile_list.shape[0]
    their_frame, place = tile_list // frame_tiles, tile_list % frame_tiles
    step = their_frame - frame
    slot = 1 - jnp.where(frame % 2 == 0, step, -step)
    local_list = slot * frame_tiles + place
    result = attend(local_list, first, rest, near, kv, far)
    return merge_heads(exchange(result))


def solution(mesh):
    in_specs = (P(("blk", "uly"), None), P("blk", None))
    out_specs = P(("blk", "uly"), None)
    return jax.shard_map(
        on_device, mesh=mesh, in_specs=in_specs, out_specs=out_specs, check_vma=False
    )
```

```python
import jax
import jax.numpy as jnp
from jax import lax
from jax.experimental import pallas as pl
from jax.experimental.pallas import tpu as pltpu
from jax.sharding import PartitionSpec as P

HEAD_DIM = 64
PAIR = 2 * HEAD_DIM
SPLIT_HEADS = 16
STEP_TILES = 16
FIRST_ROWS = 8
SPLIT_CHUNK = 8
SPLIT_VMEM = 57 * 2**20


def split_kernel(qkv_ref, kv_ref, q_ref, landed, packed, sems, q_sems):
    chunks, tokens, width = landed.shape
    half = tokens // 2
    copies = [
        pltpu.make_async_copy(qkv_ref.at[:, pl.ds(i * width, width)], landed.at[i], sems.at[i])
        for i in range(chunks)
    ]
    for copy in copies:
        copy.start()
    heads = width // (3 * HEAD_DIM)
    q_copies = []
    for i in range(chunks):
        copies[i].wait()
        for j in range(heads):
            col = j * 3 * HEAD_DIM
            head = i * heads + j
            kv_ref[head] = landed[i, :, col + HEAD_DIM : col + 3 * HEAD_DIM]
            packed[head] = jnp.concatenate(
                [landed[i, :half, col : col + HEAD_DIM], landed[i, half:, col : col + HEAD_DIM]], axis=1
            )
        part = pl.ds(i * heads, heads)
        q_copies.append(pltpu.make_async_copy(packed.at[part], q_ref.at[part], q_sems.at[i]))
        q_copies[i].start()
    for copy in q_copies:
        copy.wait()


def split_heads(qkv):
    tokens, width = qkv.shape
    heads = width // (3 * HEAD_DIM)
    chunks = heads // SPLIT_CHUNK
    return pl.pallas_call(
        split_kernel,
        in_specs=[pl.BlockSpec(memory_space=pltpu.HBM)],
        out_specs=[pl.BlockSpec(memory_space=pltpu.VMEM), pl.BlockSpec(memory_space=pltpu.HBM)],
        out_shape=[
            pltpu.VMEM((heads, tokens, PAIR), qkv.dtype),
            pltpu.HBM((heads, tokens // 2, PAIR), qkv.dtype),
        ],
        scratch_shapes=[
            pltpu.VMEM((chunks, tokens, width // chunks), qkv.dtype),
            pltpu.VMEM((heads, tokens // 2, PAIR), qkv.dtype),
            pltpu.SemaphoreType.DMA((chunks,)),
            pltpu.SemaphoreType.DMA((chunks,)),
        ],
        compiler_params=pltpu.CompilerParams(vmem_limit_bytes=SPLIT_VMEM),
        name="split_heads",
    )(qkv)


def merge_kernel(o_ref, out_ref):
    half = o_ref.shape[1]
    for pair in range(o_ref.shape[0] // 2):
        even = o_ref[2 * pair]
        odd = o_ref[2 * pair + 1]
        cols = slice(pair * PAIR, (pair + 1) * PAIR)
        out_ref[:half, cols] = jnp.concatenate([even[:, :HEAD_DIM], odd[:, :HEAD_DIM]], axis=1)
        out_ref[half:, cols] = jnp.concatenate([even[:, HEAD_DIM:], odd[:, HEAD_DIM:]], axis=1)


def merge_heads(parts):
    heads, half, _ = parts.shape
    group = SPLIT_HEADS
    return pl.pallas_call(
        merge_kernel,
        grid=(heads // group,),
        in_specs=[pl.BlockSpec((group, half, PAIR), lambda i: (i, 0, 0))],
        out_specs=pl.BlockSpec((2 * half, group * HEAD_DIM), lambda i: (0, i)),
        out_shape=jax.ShapeDtypeStruct((2 * half, heads * HEAD_DIM), parts.dtype),
        compiler_params=pltpu.CompilerParams(vmem_limit_bytes=8 * 2**20),
        name="merge_heads",
    )(parts)


def load_all(pairs, sems):
    copies = [pltpu.make_async_copy(src, dst, sems.at[i]) for i, (src, dst) in enumerate(pairs)]
    for copy in copies:
        copy.start()
    for copy in copies:
        copy.wait()


def padded_query(packed):
    packed = packed * jnp.bfloat16(HEAD_DIM**-0.5)
    stacked = jnp.concatenate([packed[:, :HEAD_DIM], packed[:, HEAD_DIM:]], axis=0)
    return jnp.concatenate([stacked, jnp.zeros_like(stacked)], axis=1)


def attend_kernel(list_ref, q_ref, prev_ref, own_ref, next_ref, o_ref, asked, raw, sems):
    step = pl.program_id(0)

    @pl.when(step == 0)
    def _():
        tiles = own_ref.shape[0]
        pairs = [
            (src, raw.at[pl.ds(i * tiles, tiles)])
            for i, src in enumerate((prev_ref, own_ref, next_ref))
        ]
        pairs.append((q_ref, asked))
        load_all(pairs, sems)

    count = list_ref.shape[1]

    def score(u):
        tile = step * o_ref.shape[0] + u
        query = padded_query(asked[tile])
        listed = [list_ref[tile, j] for j in range(count)]
        dims = (((1,), (1,)), ((), ()))
        scores = [
            lax.dot_general(query, raw[t], dims, preferred_element_type=jnp.float32) for t in listed
        ]
        return listed, scores

    def finish(u, listed, scores):
        top = scores[0]
        for s in scores[1:]:
            top = jnp.maximum(top, s)
        row_max = jnp.max(top, axis=1, keepdims=True)
        total = None
        for s, t in zip(scores, listed):
            weights = jnp.exp(s - row_max).astype(jnp.bfloat16)
            kv = raw[t]
            low = lax.broadcasted_iota(jnp.int32, kv.shape, 1) < HEAD_DIM
            ones_values = jnp.where(low, jnp.ones_like(kv), kv)
            part = jnp.dot(weights, ones_values, preferred_element_type=jnp.float32)
            total = part if total is None else total + part
        out = (total[:, HEAD_DIM:] / total[:, :HEAD_DIM]).astype(o_ref.dtype)
        half = out.shape[0] // 2
        o_ref[u] = jnp.concatenate([out[:half], out[half:]], axis=1)

    held = score(0)
    for u in range(o_ref.shape[0]):
        following = score(u + 1) if u + 1 < o_ref.shape[0] else None
        finish(u, *held)
        held = following


def attend(local_list, queries, before, own, after):
    tiles, half, _ = queries.shape
    tile_len = own.shape[1]
    hbm = pl.BlockSpec(memory_space=pl.ANY)
    return pl.pallas_call(
        attend_kernel,
        grid_spec=pltpu.PrefetchScalarGridSpec(
            num_scalar_prefetch=1,
            grid=(tiles // STEP_TILES,),
            in_specs=[hbm] * 4,
            out_specs=pl.BlockSpec((STEP_TILES, half, PAIR), lambda i, _: (i, 0, 0)),
            scratch_shapes=[
                pltpu.VMEM((tiles, half, PAIR), jnp.bfloat16),
                pltpu.VMEM((3 * tiles, tile_len, PAIR), jnp.bfloat16),
                pltpu.SemaphoreType.DMA((4,)),
            ],
        ),
        out_shape=jax.ShapeDtypeStruct((tiles, half, PAIR), queries.dtype),
        compiler_params=pltpu.CompilerParams(vmem_limit_bytes=32 * 2**20),
        name="attend",
    )(local_list, queries, before, own, after)


def exchange(array):
    return lax.all_to_all(array, "uly", split_axis=0, concat_axis=0, tiled=True)


def exchange_in_two(array):
    first = exchange(array[:, :FIRST_ROWS])
    array, first = lax.optimization_barrier((array, first))
    return jnp.concatenate([first, exchange(array[:, FIRST_ROWS:])], axis=1)


def late_frame(frame):
    return (frame + 1) // 2 % 2


def on_device(qkv, tile_list):
    frames = lax.axis_size("blk")
    frame = lax.axis_index("blk")
    kv, queries = split_heads(qkv)
    kv = lax.cond(late_frame(frame) == 0, exchange, exchange_in_two, kv)
    far = lax.ppermute(kv, "blk", [p for i in range(1, frames - 1, 2) for p in ((i, i + 1), (i + 1, i))])
    queries = exchange(queries)
    near = lax.ppermute(kv, "blk", [p for i in range(0, frames, 2) for p in ((i, i + 1), (i + 1, i))])
    far, queries, tile_list = lax.optimization_barrier((far, queries, tile_list))
    frame_tiles = tile_list.shape[0]
    their_frame, place = tile_list // frame_tiles, tile_list % frame_tiles
    step = their_frame - frame
    slot = 1 - jnp.where(frame % 2 == 0, step, -step)
    local_list = slot * frame_tiles + place
    result = attend(local_list, queries, near, kv, far)
    return merge_heads(exchange(result))


def solution(mesh):
    in_specs = (P(("blk", "uly"), None), P("blk", None))
    out_specs = P(("blk", "uly"), None)
    return jax.shard_map(
        on_device, mesh=mesh, in_specs=in_specs, out_specs=out_specs, check_vma=False
    )
```

```python
import jax
import jax.numpy as jnp
from jax import lax
from jax.experimental import pallas as pl
from jax.experimental.pallas import tpu as pltpu
from jax.sharding import PartitionSpec as P

HEAD_DIM = 64
PAIR = 2 * HEAD_DIM
SPLIT_HEADS = 16
STEP_TILES = 16
FIRST_ROWS = 8


def split_kernel(qkv_ref, kv_ref, q_ref):
    half = qkv_ref.shape[0] // 2
    for pair in range(kv_ref.shape[0] // 2):
        base = pair * 6 * HEAD_DIM
        for odd in range(2):
            col = base + odd * 3 * HEAD_DIM
            head = 2 * pair + odd
            kv_ref[head] = qkv_ref[:, col + HEAD_DIM : col + 3 * HEAD_DIM]
            q_ref[head] = jnp.concatenate(
                [qkv_ref[:half, col : col + HEAD_DIM], qkv_ref[half:, col : col + HEAD_DIM]], axis=1
            )


def split_heads(qkv):
    tokens, width = qkv.shape
    heads = width // (3 * HEAD_DIM)
    group = SPLIT_HEADS
    return pl.pallas_call(
        split_kernel,
        grid=(heads // group,),
        in_specs=[pl.BlockSpec((tokens, group * 3 * HEAD_DIM), lambda i: (0, i))],
        out_specs=[
            pl.BlockSpec((group, tokens, PAIR), lambda i: (i, 0, 0)),
            pl.BlockSpec((group, tokens // 2, PAIR), lambda i: (i, 0, 0)),
        ],
        out_shape=[
            jax.ShapeDtypeStruct((heads, tokens, PAIR), qkv.dtype),
            jax.ShapeDtypeStruct((heads, tokens // 2, PAIR), qkv.dtype),
        ],
        name="split_heads",
    )(qkv)


def merge_kernel(o_ref, out_ref):
    half = o_ref.shape[1]
    for pair in range(o_ref.shape[0] // 2):
        even = o_ref[2 * pair]
        odd = o_ref[2 * pair + 1]
        cols = slice(pair * PAIR, (pair + 1) * PAIR)
        out_ref[:half, cols] = jnp.concatenate([even[:, :HEAD_DIM], odd[:, :HEAD_DIM]], axis=1)
        out_ref[half:, cols] = jnp.concatenate([even[:, HEAD_DIM:], odd[:, HEAD_DIM:]], axis=1)


def merge_heads(parts):
    heads, half, _ = parts.shape
    group = SPLIT_HEADS
    return pl.pallas_call(
        merge_kernel,
        grid=(heads // group,),
        in_specs=[pl.BlockSpec((group, half, PAIR), lambda i: (i, 0, 0))],
        out_specs=pl.BlockSpec((2 * half, group * HEAD_DIM), lambda i: (0, i)),
        out_shape=jax.ShapeDtypeStruct((2 * half, heads * HEAD_DIM), parts.dtype),
        compiler_params=pltpu.CompilerParams(vmem_limit_bytes=8 * 2**20),
        name="merge_heads",
    )(parts)


def load_all(pairs, sems):
    copies = [pltpu.make_async_copy(src, dst, sems.at[i]) for i, (src, dst) in enumerate(pairs)]
    for copy in copies:
        copy.start()
    for copy in copies:
        copy.wait()


def padded_query(packed):
    packed = packed * jnp.bfloat16(HEAD_DIM**-0.5)
    stacked = jnp.concatenate([packed[:, :HEAD_DIM], packed[:, HEAD_DIM:]], axis=0)
    return jnp.concatenate([stacked, jnp.zeros_like(stacked)], axis=1)


def attend_kernel(list_ref, q_ref, prev_ref, own_ref, next_ref, o_ref, asked, raw, sems):
    step = pl.program_id(0)

    @pl.when(step == 0)
    def _():
        tiles = own_ref.shape[0]
        pairs = [
            (src, raw.at[pl.ds(i * tiles, tiles)])
            for i, src in enumerate((prev_ref, own_ref, next_ref))
        ]
        pairs.append((q_ref, asked))
        load_all(pairs, sems)

    count = list_ref.shape[1]

    def score(u):
        tile = step * o_ref.shape[0] + u
        query = padded_query(asked[tile])
        listed = [list_ref[tile, j] for j in range(count)]
        dims = (((1,), (1,)), ((), ()))
        scores = [
            lax.dot_general(query, raw[t], dims, preferred_element_type=jnp.float32) for t in listed
        ]
        return listed, scores

    def finish(u, listed, scores):
        top = scores[0]
        for s in scores[1:]:
            top = jnp.maximum(top, s)
        row_max = jnp.max(top, axis=1, keepdims=True)
        total = None
        for s, t in zip(scores, listed):
            weights = jnp.exp(s - row_max).astype(jnp.bfloat16)
            kv = raw[t]
            low = lax.broadcasted_iota(jnp.int32, kv.shape, 1) < HEAD_DIM
            ones_values = jnp.where(low, jnp.ones_like(kv), kv)
            part = jnp.dot(weights, ones_values, preferred_element_type=jnp.float32)
            total = part if total is None else total + part
        out = (total[:, HEAD_DIM:] / total[:, :HEAD_DIM]).astype(o_ref.dtype)
        half = out.shape[0] // 2
        o_ref[u] = jnp.concatenate([out[:half], out[half:]], axis=1)

    held = score(0)
    for u in range(o_ref.shape[0]):
        following = score(u + 1) if u + 1 < o_ref.shape[0] else None
        finish(u, *held)
        held = following


def attend(local_list, queries, before, own, after):
    tiles, half, _ = queries.shape
    tile_len = own.shape[1]
    hbm = pl.BlockSpec(memory_space=pl.ANY)
    return pl.pallas_call(
        attend_kernel,
        grid_spec=pltpu.PrefetchScalarGridSpec(
            num_scalar_prefetch=1,
            grid=(tiles // STEP_TILES,),
            in_specs=[hbm] * 4,
            out_specs=pl.BlockSpec((STEP_TILES, half, PAIR), lambda i, _: (i, 0, 0)),
            scratch_shapes=[
                pltpu.VMEM((tiles, half, PAIR), jnp.bfloat16),
                pltpu.VMEM((3 * tiles, tile_len, PAIR), jnp.bfloat16),
                pltpu.SemaphoreType.DMA((4,)),
            ],
        ),
        out_shape=jax.ShapeDtypeStruct((tiles, half, PAIR), queries.dtype),
        compiler_params=pltpu.CompilerParams(vmem_limit_bytes=32 * 2**20),
        name="attend",
    )(local_list, queries, before, own, after)


def exchange(array):
    return lax.all_to_all(array, "uly", split_axis=0, concat_axis=0, tiled=True)


def join_kernel(first_ref, rest_ref, out_ref, sems):
    rows = first_ref.shape[1]
    pairs = [
        (first_ref, out_ref.at[:, pl.ds(0, rows)]),
        (rest_ref, out_ref.at[:, pl.ds(rows, rest_ref.shape[1])]),
    ]
    load_all(pairs, sems)


def join_rows(first, rest):
    hbm = pl.BlockSpec(memory_space=pl.ANY)
    rows = first.shape[1] + rest.shape[1]
    return pl.pallas_call(
        join_kernel,
        in_specs=[hbm, hbm],
        out_specs=hbm,
        out_shape=jax.ShapeDtypeStruct((first.shape[0], rows, first.shape[2]), first.dtype),
        scratch_shapes=[pltpu.SemaphoreType.DMA((2,))],
        compiler_params=pltpu.CompilerParams(vmem_limit_bytes=2**20),
        name="join_rows",
    )(first, rest)


def exchange_in_two(array):
    first = exchange(array[:, :FIRST_ROWS])
    array, first = lax.optimization_barrier((array, first))
    return join_rows(first, exchange(array[:, FIRST_ROWS:]))


def late_frame(frame):
    return (frame + 1) // 2 % 2


def on_device(qkv, tile_list):
    frames = lax.axis_size("blk")
    frame = lax.axis_index("blk")
    kv, queries = split_heads(qkv)
    kv = lax.cond(late_frame(frame) == 0, exchange, exchange_in_two, kv)
    far = lax.ppermute(kv, "blk", [p for i in range(1, frames - 1, 2) for p in ((i, i + 1), (i + 1, i))])
    queries = exchange(queries)
    near = lax.ppermute(kv, "blk", [p for i in range(0, frames, 2) for p in ((i, i + 1), (i + 1, i))])
    far, queries, tile_list = lax.optimization_barrier((far, queries, tile_list))
    frame_tiles = tile_list.shape[0]
    their_frame, place = tile_list // frame_tiles, tile_list % frame_tiles
    step = their_frame - frame
    slot = 1 - jnp.where(frame % 2 == 0, step, -step)
    local_list = slot * frame_tiles + place
    result = attend(local_list, queries, near, kv, far)
    return merge_heads(exchange(result))


def solution(mesh):
    in_specs = (P(("blk", "uly"), None), P("blk", None))
    out_specs = P(("blk", "uly"), None)
    return jax.shard_map(
        on_device, mesh=mesh, in_specs=in_specs, out_specs=out_specs, check_vma=False
    )
```

```python
import jax
import jax.numpy as jnp
from jax import lax
from jax.experimental import pallas as pl
from jax.experimental.pallas import tpu as pltpu
from jax.sharding import PartitionSpec as P

HEAD_DIM = 64
PAIR = 2 * HEAD_DIM
SPLIT_HEADS = 16
STEP_TILES = 16
FIRST_ROWS = 8


def split_kernel(qkv_ref, kv_ref, q_ref):
    half = qkv_ref.shape[0] // 2
    for pair in range(kv_ref.shape[0] // 2):
        base = pair * 6 * HEAD_DIM
        for odd in range(2):
            col = base + odd * 3 * HEAD_DIM
            head = 2 * pair + odd
            kv_ref[head] = qkv_ref[:, col + HEAD_DIM : col + 3 * HEAD_DIM]
            q_ref[head] = jnp.concatenate(
                [qkv_ref[:half, col : col + HEAD_DIM], qkv_ref[half:, col : col + HEAD_DIM]], axis=1
            )


def split_heads(qkv):
    tokens, width = qkv.shape
    heads = width // (3 * HEAD_DIM)
    group = SPLIT_HEADS
    return pl.pallas_call(
        split_kernel,
        grid=(heads // group,),
        in_specs=[pl.BlockSpec((tokens, group * 3 * HEAD_DIM), lambda i: (0, i))],
        out_specs=[
            pl.BlockSpec((group, tokens, PAIR), lambda i: (i, 0, 0)),
            pl.BlockSpec((group, tokens // 2, PAIR), lambda i: (i, 0, 0)),
        ],
        out_shape=[
            jax.ShapeDtypeStruct((heads, tokens, PAIR), qkv.dtype),
            jax.ShapeDtypeStruct((heads, tokens // 2, PAIR), qkv.dtype),
        ],
        name="split_heads",
    )(qkv)


def merge_kernel(o_ref, out_ref):
    half = o_ref.shape[1]
    for pair in range(o_ref.shape[0] // 2):
        even = o_ref[2 * pair]
        odd = o_ref[2 * pair + 1]
        cols = slice(pair * PAIR, (pair + 1) * PAIR)
        out_ref[:half, cols] = jnp.concatenate([even[:, :HEAD_DIM], odd[:, :HEAD_DIM]], axis=1)
        out_ref[half:, cols] = jnp.concatenate([even[:, HEAD_DIM:], odd[:, HEAD_DIM:]], axis=1)


def merge_heads(parts):
    heads, half, _ = parts.shape
    group = SPLIT_HEADS
    return pl.pallas_call(
        merge_kernel,
        grid=(heads // group,),
        in_specs=[pl.BlockSpec((group, half, PAIR), lambda i: (i, 0, 0))],
        out_specs=pl.BlockSpec((2 * half, group * HEAD_DIM), lambda i: (0, i)),
        out_shape=jax.ShapeDtypeStruct((2 * half, heads * HEAD_DIM), parts.dtype),
        compiler_params=pltpu.CompilerParams(vmem_limit_bytes=8 * 2**20),
        name="merge_heads",
    )(parts)


def load_all(pairs, sems):
    copies = [pltpu.make_async_copy(src, dst, sems.at[i]) for i, (src, dst) in enumerate(pairs)]
    for copy in copies:
        copy.start()
    for copy in copies:
        copy.wait()


def padded_query(packed):
    packed = packed * jnp.bfloat16(HEAD_DIM**-0.5)
    stacked = jnp.concatenate([packed[:, :HEAD_DIM], packed[:, HEAD_DIM:]], axis=0)
    return jnp.concatenate([stacked, jnp.zeros_like(stacked)], axis=1)


def attend_kernel(list_ref, q_ref, prev_ref, own_ref, next_ref, o_ref, asked, raw, sems):
    step = pl.program_id(0)

    @pl.when(step == 0)
    def _():
        tiles = own_ref.shape[0]
        pairs = [
            (src, raw.at[pl.ds(i * tiles, tiles)])
            for i, src in enumerate((prev_ref, own_ref, next_ref))
        ]
        pairs.append((q_ref, asked))
        load_all(pairs, sems)

    count = list_ref.shape[1]

    def score(u):
        tile = step * o_ref.shape[0] + u
        query = padded_query(asked[tile])
        listed = [list_ref[tile, j] for j in range(count)]
        dims = (((1,), (1,)), ((), ()))
        scores = [
            lax.dot_general(query, raw[t], dims, preferred_element_type=jnp.float32) for t in listed
        ]
        return listed, scores

    def finish(u, listed, scores):
        top = scores[0]
        for s in scores[1:]:
            top = jnp.maximum(top, s)
        row_max = jnp.max(top, axis=1, keepdims=True)
        total = None
        for s, t in zip(scores, listed):
            weights = jnp.exp(s - row_max).astype(jnp.bfloat16)
            kv = raw[t]
            low = lax.broadcasted_iota(jnp.int32, kv.shape, 1) < HEAD_DIM
            ones_values = jnp.where(low, jnp.ones_like(kv), kv)
            part = jnp.dot(weights, ones_values, preferred_element_type=jnp.float32)
            total = part if total is None else total + part
        out = (total[:, HEAD_DIM:] / total[:, :HEAD_DIM]).astype(o_ref.dtype)
        half = out.shape[0] // 2
        o_ref[u] = jnp.concatenate([out[:half], out[half:]], axis=1)

    held = score(0)
    for u in range(o_ref.shape[0]):
        following = score(u + 1) if u + 1 < o_ref.shape[0] else None
        finish(u, *held)
        held = following


def attend(local_list, queries, before, own, after):
    tiles, half, _ = queries.shape
    tile_len = own.shape[1]
    hbm = pl.BlockSpec(memory_space=pl.ANY)
    return pl.pallas_call(
        attend_kernel,
        grid_spec=pltpu.PrefetchScalarGridSpec(
            num_scalar_prefetch=1,
            grid=(tiles // STEP_TILES,),
            in_specs=[hbm] * 4,
            out_specs=pl.BlockSpec((STEP_TILES, half, PAIR), lambda i, _: (i, 0, 0)),
            scratch_shapes=[
                pltpu.VMEM((tiles, half, PAIR), jnp.bfloat16),
                pltpu.VMEM((3 * tiles, tile_len, PAIR), jnp.bfloat16),
                pltpu.SemaphoreType.DMA((4,)),
            ],
        ),
        out_shape=jax.ShapeDtypeStruct((tiles, half, PAIR), queries.dtype),
        compiler_params=pltpu.CompilerParams(vmem_limit_bytes=32 * 2**20),
        name="attend",
    )(local_list, queries, before, own, after)


def exchange(array):
    return lax.all_to_all(array, "uly", split_axis=0, concat_axis=0, tiled=True)


def join_kernel(first_ref, rest_ref, out_ref, sems):
    rows = first_ref.shape[1]
    pairs = [
        (first_ref, out_ref.at[:, pl.ds(0, rows)]),
        (rest_ref, out_ref.at[:, pl.ds(rows, rest_ref.shape[1])]),
    ]
    load_all(pairs, sems)


def join_rows(first, rest):
    hbm = pl.BlockSpec(memory_space=pl.ANY)
    rows = first.shape[1] + rest.shape[1]
    return pl.pallas_call(
        join_kernel,
        in_specs=[hbm, hbm],
        out_specs=hbm,
        out_shape=jax.ShapeDtypeStruct((first.shape[0], rows, first.shape[2]), first.dtype),
        scratch_shapes=[pltpu.SemaphoreType.DMA((2,))],
        compiler_params=pltpu.CompilerParams(vmem_limit_bytes=2**20),
        name="join_rows",
    )(first, rest)


def exchange_in_two(array):
    first = exchange(array[:, :FIRST_ROWS])
    array, first = lax.optimization_barrier((array, first))
    return join_rows(first, exchange(array[:, FIRST_ROWS:]))


def late_frame(frame):
    return (frame + 3) // 2 % 2


def on_device(qkv, tile_list):
    frames = lax.axis_size("blk")
    frame = lax.axis_index("blk")
    kv, queries = split_heads(qkv)
    kv = lax.cond(late_frame(frame) == 0, exchange, exchange_in_two, kv)
    far = lax.ppermute(kv, "blk", [p for i in range(1, frames - 1, 2) for p in ((i, i + 1), (i + 1, i))])
    queries = exchange(queries)
    near = lax.ppermute(kv, "blk", [p for i in range(0, frames, 2) for p in ((i, i + 1), (i + 1, i))])
    far, queries, tile_list = lax.optimization_barrier((far, queries, tile_list))
    frame_tiles = tile_list.shape[0]
    their_frame, place = tile_list // frame_tiles, tile_list % frame_tiles
    step = their_frame - frame
    slot = 1 - jnp.where(frame % 2 == 0, step, -step)
    local_list = slot * frame_tiles + place
    result = attend(local_list, queries, near, kv, far)
    return merge_heads(exchange(result))


def solution(mesh):
    in_specs = (P(("blk", "uly"), None), P("blk", None))
    out_specs = P(("blk", "uly"), None)
    return jax.shard_map(
        on_device, mesh=mesh, in_specs=in_specs, out_specs=out_specs, check_vma=False
    )
```
